32 devices in a mesh: groups: 2 (over x), replica: 4 (over z), tensor: 4 (over y, core).
Axes of the slice: x: 2, y: 2, z: 4, core: 2. Of those that a mesh axis runs over, the one named last changes fastest.
Arguments:
- queries: bfloat16 [4096, 4096], P(('groups', 'replica'), 'tensor'), parts along dimension 0, may hold values from -8 to 8
- new_kv: bfloat16 [4096, 2, 512], P(('groups', 'replica'), None, 'tensor'), parts along dimension 0, may hold values from -6 to 6, as said below
- cache_kv: bfloat16 [16, 4096, 2, 512], P(('groups', 'replica'), None, None, 'tensor'), parts along dimension 0, may hold values from -6 to 6, as said below
- stored: int32 [8, 2], P('groups'), parts along dimension 0, may hold values from 0 to 3, as said below
- haystack_ids: int32 [64, 1], P(('groups', 'replica')), parts along dimension 0, may hold values from 0 to 3; in each aligned block of 8 rows (0 to 7, 8 to 15, ...) at most 2 rows name the same one
- token_counts: int32 [8, 8], P(('groups', 'replica')), parts along dimension 0, may hold values from 1 to 64, 384 in all within a row
- out_weight: bfloat16 [4096, 8192], P('tensor'), may hold values from -0.75 to 0.75
Outputs:
- answer: bfloat16 [4096, 8192], P(('groups', 'replica'), 'tensor'), parts along dimension 0
The draws below stay inside these ranges and needn't reach their ends.
There are 2 independent parts, one for each index of `groups`. The reference program is written for one: setup_inputs(seed, part) draws one part's arguments, and reference() takes and returns one part's arrays. A program takes and returns all parts, laid end to end along the dimension named above; an argument that names none is the same for every part. Nothing has to cross between parts.
Inputs may be any that keep to these rules, and one draw needn't show every extreme that they name: `stored`: every haystack lies in slot 0 of exactly one replica index and in slot 1 of exactly one other. `haystack_ids`: among the 8 questions of one replica index no haystack is named more than 2 times; some haystack is named exactly 2 times. `token_counts`: the counts of one replica index sum to 384 and the largest is 64. `cache_kv`: slots holding the same haystack hold equal values; the cache heads serving one kv head are equal. `new_kv`: the cache heads serving one kv head are equal.
All inputs are finite; a program needn't handle non-finite values.
Results may differ from the reference program's by a relative error of at most 0.0053.
Values may be sent and summed in bfloat16 or wider, within the bound.
No kernel may reach another device: no remote copies, remote signals or barrier semaphores. Data moves between devices by JAX's collectives and lax.ppermute only.
A program may use at most 128 MiB of HBM per device.

```python
import math
import jax
import jax.numpy as jnp
import numpy as np
from jax import lax

D = 8192
HD = 128
QH = 32
KVH = 4
QLEN = 64
SLOTS = 2
CTX = 4096
Q_DEV = 8
CAP = 2
HAYSTACKS = 4
QUESTIONS = 32
ROWS = 2048
CACHE_HEADS = 4
N_REPLICA = 4


def placement_table(key):
    base = jax.random.fold_in(key, 7)
    order = jax.random.permutation(jax.random.fold_in(base, 1), HAYSTACKS).astype(jnp.int32)
    offset = jax.random.randint(jax.random.fold_in(base, 2), (), 1, HAYSTACKS).astype(jnp.int32)
    places = jnp.arange(HAYSTACKS, dtype=jnp.int32)
    second = order[(places + offset) % HAYSTACKS]
    return jnp.stack([order, second], axis=1).astype(jnp.int32)


def draw_stored(key, part):
    return placement_table(key)


def draw_cache_kv(key, part):
    table = placement_table(key)
    base = jax.random.fold_in(key, 21)
    shape = (HAYSTACKS, CTX, 2, KVH, HD)
    content = jnp.clip(jax.random.normal(base, shape, jnp.float32), -6.0, 6.0)
    picked = content[table.reshape(-1)]
    copied = jnp.repeat(picked, CACHE_HEADS // KVH, axis=3)
    return copied.reshape(HAYSTACKS * SLOTS, CTX, 2, CACHE_HEADS * HD).astype(jnp.bfloat16)


def draw_new_kv(key, part):
    base = jax.random.fold_in(key, 41)
    shape = (ROWS, 2, KVH, HD)
    content = jnp.clip(jax.random.normal(base, shape, jnp.float32), -6.0, 6.0)
    copied = jnp.repeat(content, CACHE_HEADS // KVH, axis=2)
    return copied.reshape(ROWS, 2, CACHE_HEADS * HD).astype(jnp.bfloat16)


def draw_queries(key, part):
    base = jax.random.fold_in(key, 31)
    shape = (ROWS, QH, HD)
    content = jnp.clip(2.0 * jax.random.normal(base, shape, jnp.float32), -8.0, 8.0)
    return content.reshape(ROWS, QH * HD).astype(jnp.bfloat16)


def block_scale(stream_key, dims, shards, low, top_value):
    def one(dim, blocks):
        heights = jax.random.uniform(jax.random.fold_in(jax.random.fold_in(stream_key, 6), dim), (blocks,), jnp.float32, low / len(shards), top_value / len(shards))
        return jnp.repeat(jnp.exp(heights), dims[dim] // blocks).reshape((-1,) + (1,) * (len(dims) - dim - 1))

    level = one(*shards[0])
    for cut in shards[1:]:
        level = level * one(*cut)
    return level


def split_up(amount, total, most, lean):
    loads = [(1 << 20) // math.isqrt(rank ** lean) + 1 for rank in range(2, amount + 1)]
    rest, given = total - most - (amount - 1), [1] * (amount - 1)
    while rest > 0:
        free = [i for i in range(amount - 1) if given[i] < most]
        whole, remaining = sum([loads[i] for i in free]), rest
        for i in free:
            more = min(most - given[i], max(1, remaining * loads[i] // whole), rest)
            given[i] = given[i] + more
            rest = rest - more
    return np.array([most] + given)


def uneven_parts(stream_key, number_of, total, bound, lean):
    if number_of == 2:
        one = jax.random.randint(stream_key, (), max(1, total - bound), min(bound, total - 1) + 1)
        return jnp.stack([one, total - one])
    tallies = jnp.asarray(split_up(number_of, total, bound, lean), jnp.int32)
    twos = (number_of - 1) // 2
    donor, taker = tallies[1:1 + 2 * twos:2], tallies[2:2 + 2 * twos:2]
    margin = jnp.minimum(donor - 1, bound - taker)
    shifted = jax.random.randint(jax.random.fold_in(stream_key, 1), (twos,), 0, 1 << 20) % (margin + 1)
    tallies = tallies.at[1:1 + 2 * twos:2].set(donor - shifted).at[2:2 + 2 * twos:2].set(taker + shifted)
    return tallies[jax.random.permutation(jax.random.fold_in(stream_key, 2), number_of)]


def shared_out(key, own, number, rows, count, top, limit, slope):
    ranking = jax.random.permutation(key, count)
    crowded, ordinary = shares(count, rows * top, limit, slope, True), shares(count, rows * top, limit, slope, False)
    places = jnp.arange(count)

    def named(tallies, rotation):
        used = int((tallies > 0).sum())
        fixed = max(1, used // 4)
        moved = fixed + (places - fixed + rotation * (used - fixed)) % max(1, count - fixed)
        return jnp.zeros((count,), jnp.int32).at[ranking[jnp.where(places < fixed, places, moved)]].set(jnp.asarray(tallies, jnp.int32))

    tallies = jnp.where(number % 4 == 0, named(crowded, number // 4), named(ordinary, number - number // 4 - 1))
    mixed = jax.random.permutation(jax.random.fold_in(own, 3), count)
    giver, receiver = mixed[0:count // 2 * 2:2], mixed[1:count // 2 * 2:2]
    room = jnp.minimum(tallies[giver] - 1, limit - tallies[receiver]) // 2
    room = jnp.where((giver == ranking[0]) | (receiver == ranking[0]) | (tallies[receiver] == 0), 0, jnp.maximum(room, 0))
    moved = jax.random.randint(jax.random.fold_in(own, 4), (count // 2,), 0, 1 << 20) % (room + 1)
    tallies = tallies.at[giver].add(-moved).at[receiver].add(moved)
    labels = jnp.searchsorted(jnp.cumsum(tallies), jnp.arange(rows * top), side="right").astype(jnp.int32)
    table = labels.reshape(top, rows).T
    table = table[jax.random.permutation(jax.random.fold_in(own, 1), rows)]
    rotation = jax.random.randint(jax.random.fold_in(own, 2), (rows, 1), 0, top)
    return jnp.take_along_axis(table, (jnp.arange(top)[None, :] + rotation) % top, axis=1)


def shares(count, total, reach, slope, full):
    loads = [(1 << 20) // math.isqrt(standing ** slope) + 1 for standing in range(1, count + 1)]
    largest = reach if full else min(reach, max(-(-total // count), total * loads[0] // sum(loads)))
    least = 1 if total - largest >= count - 1 else 0
    given, spare = [largest] + [least] * (count - 1), total - largest - least * (count - 1)
    while spare > 0:
        candidates = [i for i in range(1, count) if given[i] < largest] or [i for i in range(1, count) if given[i] < reach]
        pool, left = sum([loads[i] for i in candidates]), spare
        for i in candidates:
            addition = min(reach - given[i], max(1, left * loads[i] // pool), spare)
            given[i] = given[i] + addition
            spare = spare - addition
    return np.array(given)


def scatter_about(rng, dims, deviation, most, shards=(), kind=jnp.bfloat16):
    values = jax.random.normal(rng, dims, jnp.float32) * deviation
    if len(shards) > 0:
        values = block_scale(rng, dims, shards, -0.22, 0.18) * values
    return jnp.clip(values, min=-most, max=most).astype(kind)


def setup_inputs(seed: int = 0, part: int = 0) -> dict:
    arg_keys = jax.random.split(jax.random.key(seed), 8)
    own_keys = jax.random.split(jax.random.fold_in(arg_keys[7], part), 8)
    queries = draw_queries(jax.random.fold_in(jax.random.fold_in(arg_keys[7], part), 71), part)
    new_kv = draw_new_kv(jax.random.fold_in(jax.random.fold_in(arg_keys[7], part), 71), part)
    cache_kv = draw_cache_kv(jax.random.fold_in(jax.random.fold_in(arg_keys[7], part), 71), part)
    stored = draw_stored(jax.random.fold_in(jax.random.fold_in(arg_keys[7], part), 71), part)
    haystack_ids_keys = jax.random.split(jax.random.fold_in(own_keys[4], 1), QUESTIONS // Q_DEV)
    haystack_ids_turns = jax.random.permutation(jax.random.fold_in(own_keys[4], 3), QUESTIONS // Q_DEV)
    haystack_ids = jax.vmap(lambda own, number: shared_out(jax.random.fold_in(own_keys[4], 2), own, number, Q_DEV, HAYSTACKS, 1, CAP, 2))(haystack_ids_keys, haystack_ids_turns).reshape((QUESTIONS, 1))
    token_counts = jax.vmap(lambda own: uneven_parts(own, Q_DEV, 3 * Q_DEV * QLEN // 4, QLEN, 1))(jax.random.split(own_keys[5], N_REPLICA)).reshape((N_REPLICA, Q_DEV)).astype(jnp.int32)
    out_weight = scatter_about(arg_keys[6], (QH * HD, D), (QH * HD // 64) ** -0.5, 0.75, ((0, 4),))
    return {"queries": queries, "new_kv": new_kv, "cache_kv": cache_kv, "stored": stored, "haystack_ids": haystack_ids, "token_counts": token_counts, "out_weight": out_weight}


def attend_one(query_rows, own_rows, cache_one, count):
    repeat = CACHE_HEADS // KVH
    group = QH // KVH
    cache_heads = cache_one.reshape(CTX, 2, KVH, repeat, HD)[:, :, :, 0].astype(jnp.float32)
    own_heads = own_rows.reshape(QLEN, 2, KVH, repeat, HD)[:, :, :, 0].astype(jnp.float32)
    query = query_rows.reshape(QLEN, KVH, group, HD).astype(jnp.float32)
    scale = 1.0 / math.sqrt(HD)
    far = jnp.einsum('tkgd,jkd->kgtj', query, cache_heads[:, 0]) * scale
    near = jnp.einsum('tkgd,ukd->kgtu', query, own_heads[:, 0]) * scale
    causal = jnp.arange(QLEN)[:, None] >= jnp.arange(QLEN)[None, :]
    near = jnp.where(causal[None, None], near, -jnp.inf)
    top = jnp.maximum(lax.optimization_barrier(jnp.max(far, axis=-1)), lax.optimization_barrier(jnp.max(near, axis=-1)))
    far_exp = jnp.exp(far - top[..., None])
    near_exp = jnp.exp(near - top[..., None])
    total = lax.optimization_barrier(jnp.sum(far_exp, axis=-1)) + lax.optimization_barrier(jnp.sum(near_exp, axis=-1))
    far_weight = lax.optimization_barrier(far_exp.astype(jnp.bfloat16)).astype(jnp.float32)
    near_weight = lax.optimization_barrier(near_exp.astype(jnp.bfloat16)).astype(jnp.float32)
    mixed = jnp.einsum('kgtj,jkd->tkgd', far_weight, cache_heads[:, 1])
    mixed = mixed + jnp.einsum('kgtu,ukd->tkgd', near_weight, own_heads[:, 1])
    result = mixed / jnp.transpose(total, (2, 0, 1))[..., None]
    result = result.reshape(QLEN, QH * HD)
    used = jnp.arange(QLEN)[:, None] < count
    return jnp.where(used, result, 0.0).astype(jnp.bfloat16)

def reference(queries, new_kv, cache_kv, stored, haystack_ids, token_counts, out_weight):
    flat_slots = stored.reshape(-1)
    counts = token_counts.reshape(-1)
    query_all = queries.reshape(QUESTIONS, QLEN, QH * HD)
    own_all = new_kv.reshape(QUESTIONS, QLEN, 2, CACHE_HEADS * HD)

    def one_question(items):
        query_rows, own_rows, haystack, count = items
        slot_index = jnp.argmax((flat_slots == haystack).astype(jnp.int32)).astype(jnp.int32)
        cache_one = lax.dynamic_index_in_dim(cache_kv, slot_index, 0, keepdims=False)
        return attend_one(query_rows, own_rows, cache_one, count)
    attended = lax.map(one_question, (query_all, own_all, haystack_ids[:, 0], counts))
    attended = attended.reshape(ROWS, QH * HD)
    return jnp.dot(attended, out_weight, preferred_element_type=jnp.float32).astype(jnp.bfloat16)
```

```python
import functools
import math

import jax
import jax.numpy as jnp
from jax import lax
from jax.experimental import pallas as pl
from jax.experimental.pallas import tpu as pltpu
from jax.sharding import PartitionSpec as P

CAP = 2
BF16 = jnp.bfloat16
F32 = jnp.float32
LOG2E = 1.4426950408889634
TOTAL_MAX = 1e30


def pack_kernel(stored_ref, ids_ref, q_ref, own_ref, table_ref, *out_refs, questions, heads, qlength):
    replicas = len(out_refs)
    head_size = own_ref.shape[1]
    me = lax.axis_index("replica")
    for s, out_ref in enumerate(out_refs):
        haystack = stored_ref[lax.rem(me + s, replicas), 0]
        count = jnp.int32(0)
        found = [jnp.int32(-1)] * CAP
        for i in range(questions):
            hit = ids_ref[i, 0] == haystack
            for j in range(CAP):
                found[j] = jnp.where(hit & (count == j), jnp.int32(i), found[j])
            count = count + hit.astype(jnp.int32)
        for j in range(CAP):
            table_ref[s * CAP + j] = found[j]
            place = jnp.maximum(found[j], 0)
            rows = q_ref[pl.ds(pl.multiple_of(place * qlength, qlength), qlength), :]
            for h in range(heads):
                out_ref[j, h * qlength : (h + 1) * qlength, :] = rows[:, h * head_size : (h + 1) * head_size]
            own = own_ref[pl.ds(pl.multiple_of(place * 2 * qlength, 2 * qlength), 2 * qlength), :]
            out_ref[j, heads * qlength :, :] = own


def pack(stored, ids, queries, own, replicas):
    questions = ids.shape[0]
    head_size = own.shape[1]
    qlength = queries.shape[0] // questions
    heads = queries.shape[1] // head_size
    rows = heads * qlength + 2 * qlength
    smem = pl.BlockSpec(memory_space=pltpu.SMEM)
    vmem = pl.BlockSpec(memory_space=pltpu.VMEM)
    out = pl.pallas_call(
        functools.partial(pack_kernel, questions=questions, heads=heads, qlength=qlength),
        in_specs=[smem, smem, vmem, vmem],
        out_specs=[smem] + [vmem] * replicas,
        out_shape=[jax.ShapeDtypeStruct((replicas * CAP,), jnp.int32)]
        + [jax.ShapeDtypeStruct((CAP, rows, head_size), BF16)] * replicas,
        cost_estimate=pl.CostEstimate(flops=0, bytes_accessed=4 << 20, transcendentals=0),
        name="pack",
    )(stored, ids, queries, own)
    return out[0], out[1:]


def attend_kernel(x_ref, k_ref, vt_ref, o_ref, *, heads, qlength):
    context, head_size = k_ref.shape
    scale = LOG2E / math.sqrt(head_size)
    rows = heads * qlength
    qt = x_ref[0, :rows, :].T
    own = x_ref[0, rows:, :]
    near = jnp.dot(own, qt, preferred_element_type=F32) * scale
    u2 = lax.broadcasted_iota(jnp.int32, near.shape, 0)
    t = lax.broadcasted_iota(jnp.int32, near.shape, 1) % qlength
    valid = (u2 % 2 == 0) & (u2 <= 2 * t)
    near = jnp.where(valid, near, -jnp.inf)
    near_top = jnp.max(near, axis=0, keepdims=True)
    own_t = own.astype(F32).T.astype(BF16)
    ones = jnp.ones((16, context), BF16)
    vt = jnp.concatenate([vt_ref[...], ones], axis=0)
    own_vt = jnp.concatenate([own_t, ones[:, : 2 * qlength]], axis=0)

    def mix(top, far_weights):
        near_weights = pltpu.roll(jnp.exp2(near - top), 1, 0).astype(BF16)
        mixed = jnp.dot(vt, far_weights, preferred_element_type=F32)
        return mixed + jnp.dot(own_vt, near_weights, preferred_element_type=F32)

    def store(mixed):
        result = (mixed[:head_size] / mixed[head_size : head_size + 1]).T.astype(BF16)
        for h in range(heads):
            o_ref[:, h * head_size : (h + 1) * head_size] = result[h * qlength : (h + 1) * qlength, :]

    def far_scores():
        return jnp.dot(k_ref[...], qt, preferred_element_type=F32) * scale

    mixed = mix(near_top, jnp.exp2(far_scores() - near_top).astype(BF16))
    store(mixed)
    total = jnp.max(mixed[head_size : head_size + 1])

    @pl.when(jnp.logical_not(total < TOTAL_MAX))
    def _():
        scores = far_scores()
        top = jnp.maximum(near_top, jnp.max(scores, axis=0, keepdims=True))
        store(mix(top, jnp.exp2(scores - top).astype(BF16)))


def attend(x, keys, values_t, heads, qlength):
    number, rows, head_size = x.shape
    context = keys.shape[0]
    width = heads * head_size
    return pl.pallas_call(
        functools.partial(attend_kernel, heads=heads, qlength=qlength),
        grid=(number,),
        in_specs=[
            pl.BlockSpec((1, rows, head_size), lambda i: (i, 0, 0)),
            pl.BlockSpec((context, head_size), lambda i: (0, 0)),
            pl.BlockSpec((head_size, context), lambda i: (0, 0)),
        ],
        out_specs=pl.BlockSpec((qlength, width), lambda i: (i, 0)),
        out_shape=jax.ShapeDtypeStruct((number * qlength, width), BF16),
        cost_estimate=pl.CostEstimate(
            flops=8 * number * qlength * heads * context * head_size,
            bytes_accessed=4 << 20,
            transcendentals=number * qlength * heads * context,
        ),
        name="attend",
    )(x, keys, values_t)


def project_kernel(me_ref, a_ref, w_ref, give_ref, keep_ref, *, tiles):
    product = jnp.dot(a_ref[...], w_ref[...], preferred_element_type=F32)

    @pl.when(pl.program_id(0) < tiles)
    def _():
        give_ref[...] = product.astype(give_ref.dtype)

    @pl.when(pl.program_id(0) >= tiles)
    def _():
        keep_ref[...] = product


def project(me, rows, weight, flip, shares, tile):
    number, depth = rows.shape
    columns = weight.shape[1] // shares
    tiles = columns // tile

    def weight_map(i, me_ref):
        block = me_ref[0] ^ flip ^ (i < tiles).astype(jnp.int32)
        return 0, block * tiles + lax.rem(i, tiles)

    return pl.pallas_call(
        functools.partial(project_kernel, tiles=tiles),
        grid_spec=pltpu.PrefetchScalarGridSpec(
            num_scalar_prefetch=1,
            grid=(2 * tiles,),
            in_specs=[
                pl.BlockSpec((number, depth), lambda i, me_ref: (0, 0)),
                pl.BlockSpec((depth, tile), weight_map),
            ],
            out_specs=[
                pl.BlockSpec((number, tile), lambda i, me_ref: (0, jnp.minimum(i, tiles - 1))),
                pl.BlockSpec((number, tile), lambda i, me_ref: (0, jnp.maximum(i - tiles, 0))),
            ],
        ),
        out_shape=[
            jax.ShapeDtypeStruct((number, columns), BF16),
            jax.ShapeDtypeStruct((number, columns), F32),
        ],
        cost_estimate=pl.CostEstimate(
            flops=4 * number * depth * columns, bytes_accessed=4 * depth * columns, transcendentals=0
        ),
        name="project",
    )(me, rows, weight)


def finish_kernel(table_ref, counts_ref, kept_ref, core_ref, far_ref, *refs, first):
    o_ref = refs[-1]
    place = table_ref[first + pl.program_id(0)]
    total = kept_ref[...] + core_ref[...].astype(F32) + far_ref[...].astype(F32)
    t = lax.broadcasted_iota(jnp.int32, total.shape, 0)
    o_ref[...] = jnp.where(t < counts_ref[0, place], total, 0.0).astype(o_ref.dtype)


def finish(table, counts, kept, from_core, from_far, first, previous, rows, qlength):
    number, columns = kept.shape
    block = pl.BlockSpec((qlength, columns), lambda i, table_ref, counts_ref: (i, 0))
    extra = [] if previous is None else [previous]
    return pl.pallas_call(
        functools.partial(finish_kernel, first=first),
        grid_spec=pltpu.PrefetchScalarGridSpec(
            num_scalar_prefetch=2,
            grid=(number // qlength,),
            in_specs=[block] * 3 + [pl.BlockSpec(memory_space=pl.ANY)] * len(extra),
            out_specs=pl.BlockSpec(
                (qlength, columns), lambda i, table_ref, counts_ref: (table_ref[first + i], 0)
            ),
        ),
        out_shape=jax.ShapeDtypeStruct((rows, columns), BF16),
        input_output_aliases={5: 0} if extra else {},
        cost_estimate=pl.CostEstimate(flops=0, bytes_accessed=10 * number * columns, transcendentals=0),
        name="finish",
    )(table, counts, kept, from_core, from_far, *extra)


def on_device(queries, new_kv, cache_kv, stored, haystack_ids, token_counts, out_weight):
    replicas = lax.axis_size("replica")
    shares = lax.axis_size("tensor")
    head_size = cache_kv.shape[-1]
    questions = haystack_ids.shape[0]
    rows = queries.shape[0]
    qlength = rows // questions
    heads = queries.shape[1] // head_size
    table, packed = pack(stored, haystack_ids, queries, new_kv.reshape(2 * rows, head_size), replicas)
    keys = cache_kv[0, :, 0]
    values_t = cache_kv[0, :, 1].T
    phases = sorted(range(replicas), key=lambda s: (min(s, replicas - s), s))
    arrived = {}
    for s in phases:
        arrived[s] = packed[s]
        if s:
            arrived[s] = lax.ppermute(packed[s], "replica", [(i, (i + s) % replicas) for i in range(replicas)])
    returned = {}
    for s in phases:
        result = attend(arrived[s], keys, values_t, heads, qlength)
        if s:
            result = lax.ppermute(result, "replica", [(i, (i - s) % replicas) for i in range(replicas)])
        returned[s] = result

    if shares == 4 and replicas * CAP == questions:
        me = lax.axis_index("tensor").astype(jnp.int32).reshape(1)
        other_core = [(i, i ^ 1) for i in range(shares)]
        other_chip = [(i, i ^ 2) for i in range(shares)]
        tile = 512
        out = None
        for s in phases:
            far_give, far_keep = project(me, returned[s], out_weight, 2, shares, tile)
            far_core = lax.ppermute(far_give, "tensor", other_core)
            near_give, near_keep = project(me, returned[s], out_weight, 0, shares, tile)
            near_core = lax.ppermute(near_give, "tensor", other_core)
            chip_sum = (far_keep + far_core.astype(F32)).astype(BF16)
            far = lax.ppermute(chip_sum, "tensor", other_chip)
            out = finish(table, token_counts, near_keep, near_core, far, s * CAP, out, rows, qlength)
        return out

    blocks = jnp.stack([returned[s].reshape(CAP, qlength, -1) for s in range(replicas)])
    blocks = blocks.reshape(replicas * CAP, qlength, -1)
    match = table[None, :] == jnp.arange(questions, dtype=jnp.int32)[:, None]
    position = jnp.argmax(match.astype(jnp.int32), axis=1)
    used = jnp.arange(qlength, dtype=jnp.int32)[None, :] < token_counts[0][:, None]
    attended = jnp.where(used[..., None], blocks[position], jnp.zeros((), BF16)).reshape(rows, -1)
    summed = lax.psum_scatter(
        lax.dot_general(out_weight, attended, (((0,), (1,)), ((), ())), preferred_element_type=F32),
        "tensor",
        scatter_dimension=0,
        tiled=True,
    )
    return summed.T.astype(BF16)


def solution(mesh):
    in_specs = (
        P(("groups", "replica"), "tensor"),
        P(("groups", "replica"), None, "tensor"),
        P(("groups", "replica"), None, None, "tensor"),
        P("groups", None),
        P(("groups", "replica"), None),
        P(("groups", "replica"), None),
        P("tensor", None),
    )
    out_specs = P(("groups", "replica"), "tensor")
    return jax.shard_map(
        on_device, mesh=mesh, in_specs=in_specs, out_specs=out_specs, check_vma=False
    )
```

```python
import functools
import math

import jax
import jax.numpy as jnp
from jax import lax
from jax.experimental import pallas as pl
from jax.experimental.pallas import tpu as pltpu
from jax.sharding import PartitionSpec as P


CAP = 2
BF16 = jnp.bfloat16
F32 = jnp.float32
LOG2E = 1.4426950408889634
TOTAL_MAX = 1e30
VMEM = pl.BlockSpec(memory_space=pltpu.VMEM)
SMEM = pl.BlockSpec(memory_space=pltpu.SMEM)


def pack_kernel(stored_hbm, ids_hbm, q_hbm, own_hbm, table_ref, *refs, route, heads, qlength):
    number = len(refs) - 5
    out_refs = refs[:number]
    stored_ref, ids_ref, q_ref, own_ref, sems = refs[number:]
    head_size = own_ref.shape[1]
    questions = ids_ref.shape[1]
    pairs = ((stored_hbm, stored_ref), (ids_hbm, ids_ref), (q_hbm, q_ref), (own_hbm, own_ref))
    copies = [pltpu.make_async_copy(source, target, sems.at[i]) for i, (source, target) in enumerate(pairs)]
    for copy in copies:
        copy.start()
    for copy in copies[:2]:
        copy.wait()
    places = []
    for s, haystack in enumerate(route(stored_ref, table_ref)):
        count = jnp.int32(0)
        found = [jnp.int32(-1)] * CAP
        for i in range(questions):
            hit = ids_ref[0, i] == haystack
            for j in range(CAP):
                found[j] = jnp.where(hit & (count == j), jnp.int32(i), found[j])
            count = count + hit.astype(jnp.int32)
        for j in range(CAP):
            table_ref[s * CAP + j] = found[j]
        places.append([jnp.maximum(place, 0) for place in found])
    for copy in copies[2:]:
        copy.wait()
    for s, out_ref in enumerate(out_refs):
        for j, place in enumerate(places[s]):
            rows = q_ref[pl.ds(pl.multiple_of(place * qlength, qlength), qlength), :]
            for h in range(heads):
                out_ref[j, h * qlength : (h + 1) * qlength, :] = rows[:, h * head_size : (h + 1) * head_size]
            own = own_ref[pl.ds(pl.multiple_of(place * 2 * qlength, 2 * qlength), 2 * qlength), :]
            out_ref[j, heads * qlength :, :] = own


def route_first(replicas, stored_ref, table_ref):
    me = lax.axis_index("replica")
    for s in range(replicas):
        table_ref[replicas * CAP + s] = jnp.int32(0)
    return [stored_ref[0, lax.rem(me + s, replicas)] for s in range(replicas)]


def route_near(stored_ref, table_ref):
    me = lax.axis_index("replica")

    def held(replica):
        return [stored_ref[slot, replica] for slot in range(2)]

    def plan(replica):
        here, after, before = [held(lax.rem(replica + d, 4)) for d in (0, 1, 3)]
        done = jnp.bool_(False)
        slots = [jnp.int32(0), jnp.int32(0)]
        chosen = [after[0], before[0]]
        for i in range(2):
            for k in range(2):
                one, two = after[i], before[k]
                fits = (one != here[0]) & (one != here[1]) & (two != here[0]) & (two != here[1]) & (one != two)
                take = fits & jnp.logical_not(done)
                slots = [jnp.where(take, i, slots[0]), jnp.where(take, k, slots[1])]
                chosen = [jnp.where(take, one, chosen[0]), jnp.where(take, two, chosen[1])]
                done = done | fits
        return slots, chosen, done

    plans = [plan(lax.rem(me + d, 4)) for d in range(4)]
    failed = jnp.int32(0)
    for _, _, done in plans:
        failed = jnp.where(done, failed, 1)
    table_ref[8] = jnp.int32(0)
    table_ref[9] = jnp.int32(1)
    table_ref[10] = plans[3][0][0]
    table_ref[11] = plans[1][0][1]
    table_ref[12] = failed
    return held(me) + plans[0][1]


def pack(stored, ids, queries, own, phases, route):
    questions = ids.shape[1]
    head_size = own.shape[1]
    qlength = queries.shape[0] // questions
    heads = queries.shape[1] // head_size
    rows = heads * qlength + 2 * qlength
    arguments = [pltpu.with_memory_space_constraint(x, pltpu.HBM) for x in (stored, ids, queries, own)]
    out = pl.pallas_call(
        functools.partial(pack_kernel, route=route, heads=heads, qlength=qlength),
        in_specs=[pl.BlockSpec(memory_space=pltpu.HBM)] * 4,
        out_specs=[SMEM] + [VMEM] * phases,
        out_shape=[jax.ShapeDtypeStruct((phases * (CAP + 1) + 1,), jnp.int32)]
        + [jax.ShapeDtypeStruct((CAP, rows, head_size), BF16)] * phases,
        scratch_shapes=[
            pltpu.SMEM(stored.shape, jnp.int32),
            pltpu.SMEM(ids.shape, jnp.int32),
            pltpu.VMEM(queries.shape, BF16),
            pltpu.VMEM(own.shape, BF16),
            pltpu.SemaphoreType.DMA((4,)),
        ],
        compiler_params=pltpu.CompilerParams(vmem_limit_bytes=16 << 20),
        cost_estimate=pl.CostEstimate(flops=0, bytes_accessed=4 << 20, transcendentals=0),
        name="pack",
    )(*arguments)
    return out[0], out[1:]


def split_kernel(x_ref, k_ref, vt_ref, pairs_ref, wide_ref, sems):
    parts, block, head_size = pairs_ref.shape
    half = block // 2
    slots, depth, context = vt_ref.shape
    per_slot = context // half
    copies = [
        pltpu.make_async_copy(x_ref.at[pl.ds(i * block, block), :], pairs_ref.at[i], sems.at[i]) for i in range(parts)
    ]
    for copy in copies:
        copy.start()
    vt_ref[:, head_size:, :] = jnp.ones((slots, depth - head_size, context), BF16)
    for i, copy in enumerate(copies):
        slot, place = i // per_slot, i % per_slot
        copy.wait()
        wide = wide_ref.at[i % 2]
        wide[...] = pairs_ref[i].astype(F32)
        k_ref[slot, place * half : (place + 1) * half, :] = wide[pl.ds(0, half, stride=2), :].astype(BF16)
        values = wide[pl.ds(1, half, stride=2), :]
        vt_ref[slot, :head_size, place * half : (place + 1) * half] = values.T.astype(BF16)


def split(pairs, context, slots):
    head_size = pairs.shape[1]
    per_slot = 8
    block = 2 * context // per_slot
    parts = slots * per_slot
    return pl.pallas_call(
        split_kernel,
        in_specs=[pl.BlockSpec(memory_space=pltpu.HBM)],
        out_specs=[VMEM, VMEM],
        out_shape=[
            jax.ShapeDtypeStruct((slots, context, head_size), BF16),
            jax.ShapeDtypeStruct((slots, head_size + 16, context), BF16),
        ],
        scratch_shapes=[
            pltpu.VMEM((parts, block, head_size), BF16),
            pltpu.VMEM((2, block, head_size), F32),
            pltpu.SemaphoreType.DMA((parts,)),
        ],
        compiler_params=pltpu.CompilerParams(vmem_limit_bytes=16 << 20),
        cost_estimate=pl.CostEstimate(flops=0, bytes_accessed=8 * slots * context * head_size, transcendentals=0),
        name="split",
    )(pltpu.with_memory_space_constraint(pairs, pltpu.HBM))


def attend_kernel(table_ref, x_ref, keys_ref, values_ref, o_ref, *, entry, heads, qlength, chunk):
    slot = table_ref[entry]
    k_ref, vt_ref = keys_ref.at[slot], values_ref.at[slot]
    context, head_size = k_ref.shape
    scale = LOG2E / math.sqrt(head_size)
    rows = heads * qlength

    def one(i, carry):
        qt = x_ref[i, :rows, :].T
        own = x_ref[i, rows:, :]
        near = jnp.dot(own, qt, preferred_element_type=F32) * scale
        u2 = lax.broadcasted_iota(jnp.int32, near.shape, 0)
        t = lax.broadcasted_iota(jnp.int32, near.shape, 1) % qlength
        near = jnp.where((u2 % 2 == 0) & (u2 <= 2 * t), near, -jnp.inf)
        near_top = jnp.max(near, axis=0, keepdims=True)
        own_t = own.astype(F32).T.astype(BF16)
        own_vt = jnp.concatenate([own_t, jnp.ones((16, own.shape[0]), BF16)], axis=0)

        def mix_near(top):
            weights = pltpu.roll(jnp.exp2(near - top), 1, 0).astype(BF16)
            return jnp.dot(own_vt, weights, preferred_element_type=F32)

        def store(mixed):
            result = (mixed[:head_size] / mixed[head_size : head_size + 1]).T.astype(BF16)
            for h in range(heads):
                o_ref[pl.ds(pl.multiple_of(i * qlength, qlength), qlength), h * head_size : (h + 1) * head_size] = (
                    result[h * qlength : (h + 1) * qlength, :]
                )

        scores = jnp.dot(k_ref[...], qt, preferred_element_type=F32) * scale
        weights = jnp.exp2(scores - near_top).astype(BF16)
        mixed = jnp.dot(vt_ref[...], weights, preferred_element_type=F32) + mix_near(near_top)
        store(mixed)
        total = jnp.max(mixed[head_size : head_size + 1])

        @pl.when(jnp.logical_not(total < TOTAL_MAX))
        def _():
            def part(j):
                keys = k_ref[pl.ds(pl.multiple_of(j * chunk, chunk), chunk), :]
                return jnp.dot(keys, qt, preferred_element_type=F32) * scale

            def raise_top(j, top):
                return jnp.maximum(top, jnp.max(part(j), axis=0, keepdims=True))

            top = lax.fori_loop(0, context // chunk, raise_top, near_top)

            def add(j, mixed):
                weights = jnp.exp2(part(j) - top).astype(BF16)
                values = vt_ref[:, pl.ds(pl.multiple_of(j * chunk, chunk), chunk)]
                return mixed + jnp.dot(values, weights, preferred_element_type=F32)

            store(lax.fori_loop(0, context // chunk, add, mix_near(top)))

        return carry

    lax.fori_loop(0, x_ref.shape[0], one, 0)


def attend(table, entry, x, keys, values_t, heads, qlength):
    number, _, head_size = x.shape
    context = keys.shape[1]
    return pl.pallas_call(
        functools.partial(attend_kernel, entry=entry, heads=heads, qlength=qlength, chunk=512),
        in_specs=[SMEM, VMEM, VMEM, VMEM],
        out_specs=VMEM,
        out_shape=jax.ShapeDtypeStruct((number * qlength, heads * head_size), BF16),
        compiler_params=pltpu.CompilerParams(vmem_limit_bytes=24 << 20),
        cost_estimate=pl.CostEstimate(
            flops=8 * number * qlength * heads * context * head_size,
            bytes_accessed=4 << 20,
            transcendentals=number * qlength * heads * context,
        ),
        name="attend",
    )(table, x, keys, values_t)


def project_kernel(a_ref, w_ref, give_ref, keep_ref, *, flip, tile):
    columns = keep_ref.shape[1]
    me = lax.axis_index("tensor")

    def one(i, carry):
        out = pl.ds(pl.multiple_of(i * tile, tile), tile)
        for ref, block in ((give_ref, me ^ flip ^ 1), (keep_ref, me ^ flip)):
            source = pl.ds(pl.multiple_of(block * columns + i * tile, tile), tile)
            product = jnp.dot(a_ref[...], w_ref[:, source], preferred_element_type=F32)
            ref[:, out] = product.astype(ref.dtype)
        return carry

    lax.fori_loop(0, columns // tile, one, 0)


def project(rows, weight, flip, shares, tile):
    number, depth = rows.shape
    columns = weight.shape[1] // shares
    return pl.pallas_call(
        functools.partial(project_kernel, flip=flip, tile=tile),
        in_specs=[VMEM, VMEM],
        out_specs=[VMEM, VMEM],
        out_shape=[
            jax.ShapeDtypeStruct((number, columns), BF16),
            jax.ShapeDtypeStruct((number, columns), F32),
        ],
        compiler_params=pltpu.CompilerParams(vmem_limit_bytes=12 << 20),
        cost_estimate=pl.CostEstimate(
            flops=4 * number * depth * columns, bytes_accessed=4 * depth * columns, transcendentals=0
        ),
        name="project",
    )(rows, weight)


def finish_kernel(table_ref, counts_ref, kept_ref, core_ref, far_ref, *refs, first, qlength):
    o_ref, block_ref, sems = refs[-3:]
    copies = []
    for i in range(block_ref.shape[0]):
        place = jnp.maximum(table_ref[first + i], 0)
        rows = slice(i * qlength, (i + 1) * qlength)
        total = kept_ref[rows, :] + core_ref[rows, :].astype(F32) + far_ref[rows, :].astype(F32)
        t = lax.broadcasted_iota(jnp.int32, total.shape, 0)
        block_ref[i] = jnp.where(t < counts_ref[0, place], total, 0.0).astype(BF16)
        target = o_ref.at[pl.ds(pl.multiple_of(place * qlength, qlength), qlength), :]
        copies.append(pltpu.make_async_copy(block_ref.at[i], target, sems.at[i]))
        copies[-1].start()
    for copy in copies:
        copy.wait()


def finish(table, counts, kept, from_core, from_far, first, previous, rows, qlength):
    number, columns = kept.shape[0] // qlength, kept.shape[1]
    extra = [] if previous is None else [previous]
    hbm = pl.BlockSpec(memory_space=pl.ANY)
    return pl.pallas_call(
        functools.partial(finish_kernel, first=first, qlength=qlength),
        in_specs=[SMEM, SMEM, VMEM, VMEM, VMEM] + [hbm] * len(extra),
        out_specs=hbm,
        out_shape=jax.ShapeDtypeStruct((rows, columns), BF16),
        scratch_shapes=[pltpu.VMEM((number, qlength, columns), BF16), pltpu.SemaphoreType.DMA((number,))],
        input_output_aliases={5: 0} if extra else {},
        compiler_params=pltpu.CompilerParams(vmem_limit_bytes=16 << 20),
        cost_estimate=pl.CostEstimate(flops=0, bytes_accessed=20 * number * qlength * columns, transcendentals=0),
        name="finish",
    )(table, counts, kept, from_core, from_far, *extra)


def by_shift(shift, replicas):
    return [(i, (i + shift) % replicas) for i in range(replicas)]


def small_slice(groups, replicas, shares):
    return groups <= 2 and replicas == 4 and shares == 4


def project_out(table, counts, results, weight, shares, first, out, rows, qlength):
    other_core = [(i, i ^ 1) for i in range(shares)]
    other_chip = [(i, i ^ 2) for i in range(shares)]
    tile = 512
    far_give, far_keep = project(results, weight, 2, shares, tile)
    far_core = lax.ppermute(far_give, "tensor", other_core)
    near_give, near_keep = project(results, weight, 0, shares, tile)
    near_core = lax.ppermute(near_give, "tensor", other_core)
    chip_sum = (far_keep + far_core.astype(F32)).astype(BF16)
    far = lax.ppermute(chip_sum, "tensor", other_chip)
    return finish(table, counts, near_keep, near_core, far, first, out, rows, qlength)


def answer_by_first_slots(queries, own, keys, values_t, stored, ids, heads, qlength):
    replicas = stored.shape[1]
    route = functools.partial(route_first, replicas)
    table, packed = pack(stored, ids, queries, own, replicas, route)
    arrived = [packed[0]] + [lax.ppermute(packed[s], "replica", by_shift(s, replicas)) for s in range(1, replicas)]
    result = attend(table, replicas * CAP, jnp.concatenate(arrived), keys, values_t, heads, qlength)
    parts = result.reshape(replicas, CAP * qlength, -1)
    returned = [parts[0]] + [lax.ppermute(parts[s], "replica", by_shift(-s, replicas)) for s in range(1, replicas)]
    return table, jnp.concatenate(returned)


def on_device(queries, new_kv, cache_kv, stored, haystack_ids, token_counts, out_weight):
    groups = lax.axis_size("groups")
    replicas = lax.axis_size("replica")
    shares = lax.axis_size("tensor")
    slots, context = cache_kv.shape[:2]
    head_size = cache_kv.shape[-1]
    questions = haystack_ids.shape[0]
    rows = queries.shape[0]
    qlength = rows // questions
    heads = queries.shape[1] // head_size
    own = new_kv.reshape(2 * rows, head_size)
    pairs = cache_kv.reshape(-1, head_size)
    ids = haystack_ids.T
    stored = stored.T

    if small_slice(groups, replicas, shares) and replicas * CAP == questions and slots == 2:
        table, packed = pack(stored, ids, queries, own, 4, route_near)
        arrived, returned = dict(enumerate(packed)), {}
        shifts = {2: 1, 3: -1}
        for s, shift in shifts.items():
            arrived[s] = lax.ppermute(packed[s], "replica", by_shift(shift, replicas))
        keys, values_t = split(pairs, context, slots)
        for s in range(4):
            returned[s] = attend(table, 8 + s, arrived[s], keys, values_t, heads, qlength)
            if s in shifts:
                returned[s] = lax.ppermute(returned[s], "replica", by_shift(-shifts[s], replicas))
        out = None
        for s in range(4):
            out = project_out(table, token_counts, returned[s], out_weight, shares, s * CAP, out, rows, qlength)
        failed = table[12]
        if groups == 2:
            failed = failed + lax.ppermute(failed, "groups", [(0, 1), (1, 0)])

        def again():
            keys, values_t = split(pairs, context, 1)
            table, results = answer_by_first_slots(queries, own, keys, values_t, stored, ids, heads, qlength)
            return project_out(table, token_counts, results, out_weight, shares, 0, None, rows, qlength)

        return lax.cond(failed > 0, again, lambda: out)

    keys, values_t = split(pairs, context, 1)
    table, results = answer_by_first_slots(queries, own, keys, values_t, stored, ids, heads, qlength)
    blocks = results.reshape(replicas * CAP, qlength, -1)
    match = table[None, : replicas * CAP] == jnp.arange(questions, dtype=jnp.int32)[:, None]
    position = jnp.argmax(match.astype(jnp.int32), axis=1)
    used = jnp.arange(qlength, dtype=jnp.int32)[None, :] < token_counts[0][:, None]
    attended = jnp.where(used[..., None], blocks[position], jnp.zeros((), BF16)).reshape(rows, -1)
    summed = lax.psum_scatter(
        lax.dot_general(out_weight, attended, (((0,), (1,)), ((), ())), preferred_element_type=F32),
        "tensor",
        scatter_dimension=0,
        tiled=True,
    )
    return summed.T.astype(BF16)


def solution(mesh):
    in_specs = (
        P(("groups", "replica"), "tensor"),
        P(("groups", "replica"), None, "tensor"),
        P(("groups", "replica"), None, None, "tensor"),
        P("groups", None),
        P(("groups", "replica"), None),
        P(("groups", "replica"), None),
        P("tensor", None),
    )
    out_specs = P(("groups", "replica"), "tensor")
    return jax.shard_map(
        on_device, mesh=mesh, in_specs=in_specs, out_specs=out_specs, check_vma=False
    )
```

```python
import functools
import math

import jax
import jax.numpy as jnp
from jax import lax
from jax.experimental import pallas as pl
from jax.experimental.pallas import tpu as pltpu
from jax.sharding import PartitionSpec as P


CAP = 2
BF16 = jnp.bfloat16
F32 = jnp.float32
LOG2E = 1.4426950408889634
TOTAL_MAX = 1e30
VMEM = pl.BlockSpec(memory_space=pltpu.VMEM)
SMEM = pl.BlockSpec(memory_space=pltpu.SMEM)


def pack_kernel(stored_hbm, ids_hbm, q_hbm, own_hbm, table_ref, *refs, route, heads, qlength):
    number = len(refs) - 5
    out_refs = refs[:number]
    stored_ref, ids_ref, q_ref, own_ref, sems = refs[number:]
    head_size = own_ref.shape[1]
    questions = ids_ref.shape[1]
    pairs = ((stored_hbm, stored_ref), (ids_hbm, ids_ref), (q_hbm, q_ref), (own_hbm, own_ref))
    copies = [pltpu.make_async_copy(source, target, sems.at[i]) for i, (source, target) in enumerate(pairs)]
    for copy in copies:
        copy.start()
    for copy in copies[:2]:
        copy.wait()
    places = []
    for s, haystack in enumerate(route(stored_ref, table_ref)):
        count = jnp.int32(0)
        found = [jnp.int32(-1)] * CAP
        for i in range(questions):
            hit = ids_ref[0, i] == haystack
            for j in range(CAP):
                found[j] = jnp.where(hit & (count == j), jnp.int32(i), found[j])
            count = count + hit.astype(jnp.int32)
        for j in range(CAP):
            table_ref[s * CAP + j] = found[j]
        places.append([jnp.maximum(place, 0) for place in found])
    for copy in copies[2:]:
        copy.wait()
    for s, out_ref in enumerate(out_refs):
        for j, place in enumerate(places[s]):
            rows = q_ref[pl.ds(pl.multiple_of(place * qlength, qlength), qlength), :]
            for h in range(heads):
                out_ref[j, h * qlength : (h + 1) * qlength, :] = rows[:, h * head_size : (h + 1) * head_size]
            own = own_ref[pl.ds(pl.multiple_of(place * 2 * qlength, 2 * qlength), 2 * qlength), :]
            out_ref[j, heads * qlength :, :] = own


def route_first(replicas, stored_ref, table_ref):
    me = lax.axis_index("replica")
    for s in range(replicas):
        table_ref[replicas * CAP + s] = jnp.int32(0)
    return [stored_ref[0, lax.rem(me + s, replicas)] for s in range(replicas)]


def route_near(stored_ref, table_ref):
    me = lax.axis_index("replica")

    def held(replica):
        return [stored_ref[slot, replica] for slot in range(2)]

    def plan(replica):
        here, after, before = [held(lax.rem(replica + d, 4)) for d in (0, 1, 3)]
        done = jnp.bool_(False)
        slots = [jnp.int32(0), jnp.int32(0)]
        chosen = [after[0], before[0]]
        for i in range(2):
            for k in range(2):
                one, two = after[i], before[k]
                fits = (one != here[0]) & (one != here[1]) & (two != here[0]) & (two != here[1]) & (one != two)
                take = fits & jnp.logical_not(done)
                slots = [jnp.where(take, i, slots[0]), jnp.where(take, k, slots[1])]
                chosen = [jnp.where(take, one, chosen[0]), jnp.where(take, two, chosen[1])]
                done = done | fits
        return slots, chosen, done

    plans = [plan(lax.rem(me + d, 4)) for d in range(4)]
    failed = jnp.int32(0)
    for _, _, done in plans:
        failed = jnp.where(done, failed, 1)
    table_ref[8] = jnp.int32(0)
    table_ref[9] = jnp.int32(1)
    table_ref[10] = plans[3][0][0]
    table_ref[11] = plans[1][0][1]
    table_ref[12] = failed
    return held(me) + plans[0][1]


def pack(stored, ids, queries, own, phases, route):
    questions = ids.shape[1]
    head_size = own.shape[1]
    qlength = queries.shape[0] // questions
    heads = queries.shape[1] // head_size
    rows = heads * qlength + 2 * qlength
    arguments = [pltpu.with_memory_space_constraint(x, pltpu.HBM) for x in (stored, ids, queries, own)]
    out = pl.pallas_call(
        functools.partial(pack_kernel, route=route, heads=heads, qlength=qlength),
        in_specs=[pl.BlockSpec(memory_space=pltpu.HBM)] * 4,
        out_specs=[SMEM] + [VMEM] * phases,
        out_shape=[jax.ShapeDtypeStruct((phases * (CAP + 1) + 1,), jnp.int32)]
        + [jax.ShapeDtypeStruct((CAP, rows, head_size), BF16)] * phases,
        scratch_shapes=[
            pltpu.SMEM(stored.shape, jnp.int32),
            pltpu.SMEM(ids.shape, jnp.int32),
            pltpu.VMEM(queries.shape, BF16),
            pltpu.VMEM(own.shape, BF16),
            pltpu.SemaphoreType.DMA((4,)),
        ],
        compiler_params=pltpu.CompilerParams(vmem_limit_bytes=16 << 20),
        cost_estimate=pl.CostEstimate(flops=0, bytes_accessed=4 << 20, transcendentals=0),
        name="pack",
    )(*arguments)
    return out[0], out[1:]


def split_kernel(x_ref, *refs, slot):
    k_ref, vt_ref, pairs_ref, wide_ref, sems = refs[-5:]
    parts, block, head_size = pairs_ref.shape
    half = block // 2
    depth, context = vt_ref.shape[1:]
    copies = [
        pltpu.make_async_copy(x_ref.at[pl.ds((slot * parts + i) * block, block), :], pairs_ref.at[i], sems.at[i])
        for i in range(parts)
    ]
    for copy in copies:
        copy.start()
    vt_ref[slot, head_size:, :] = jnp.ones((depth - head_size, context), BF16)
    for i, copy in enumerate(copies):
        copy.wait()
        wide = wide_ref.at[i % 2]
        wide[...] = pairs_ref[i].astype(F32)
        k_ref[slot, i * half : (i + 1) * half, :] = wide[pl.ds(0, half, stride=2), :].astype(BF16)
        values = wide[pl.ds(1, half, stride=2), :]
        vt_ref[slot, :head_size, i * half : (i + 1) * half] = values.T.astype(BF16)


def split(pairs, context, slots, slot=0, previous=None, after=None):
    head_size = pairs.shape[1]
    parts = 8
    block = 2 * context // parts
    hbm = pl.BlockSpec(memory_space=pltpu.HBM)
    extra = [] if previous is None else [*previous, after]
    return pl.pallas_call(
        functools.partial(split_kernel, slot=slot),
        in_specs=[hbm] + ([VMEM, VMEM, pl.BlockSpec(memory_space=pl.ANY)] if extra else []),
        out_specs=[VMEM, VMEM],
        out_shape=[
            jax.ShapeDtypeStruct((slots, context, head_size), BF16),
            jax.ShapeDtypeStruct((slots, head_size + 16, context), BF16),
        ],
        scratch_shapes=[
            pltpu.VMEM((parts, block, head_size), BF16),
            pltpu.VMEM((2, block, head_size), F32),
            pltpu.SemaphoreType.DMA((parts,)),
        ],
        input_output_aliases={1: 0, 2: 1} if extra else {},
        compiler_params=pltpu.CompilerParams(vmem_limit_bytes=16 << 20),
        cost_estimate=pl.CostEstimate(flops=0, bytes_accessed=8 * context * head_size, transcendentals=0),
        name="split",
    )(pltpu.with_memory_space_constraint(pairs, pltpu.HBM), *extra)


def attend_kernel(table_ref, x_ref, keys_ref, values_ref, o_ref, *, entry, heads, qlength, chunk):
    slot = table_ref[entry]
    k_ref, vt_ref = keys_ref.at[slot], values_ref.at[slot]
    context, head_size = k_ref.shape
    scale = LOG2E / math.sqrt(head_size)
    rows = heads * qlength

    def one(i, carry):
        qt = x_ref[i, :rows, :].T
        own = x_ref[i, rows:, :]
        near = jnp.dot(own, qt, preferred_element_type=F32) * scale
        u2 = lax.broadcasted_iota(jnp.int32, near.shape, 0)
        t = lax.broadcasted_iota(jnp.int32, near.shape, 1) % qlength
        near = jnp.where((u2 % 2 == 0) & (u2 <= 2 * t), near, -jnp.inf)
        near_top = jnp.max(near, axis=0, keepdims=True)
        own_t = own.astype(F32).T.astype(BF16)
        own_vt = jnp.concatenate([own_t, jnp.ones((16, own.shape[0]), BF16)], axis=0)

        def mix_near(top):
            weights = pltpu.roll(jnp.exp2(near - top), 1, 0).astype(BF16)
            return jnp.dot(own_vt, weights, preferred_element_type=F32)

        def store(mixed):
            result = (mixed[:head_size] / mixed[head_size : head_size + 1]).T.astype(BF16)
            for h in range(heads):
                o_ref[pl.ds(pl.multiple_of(i * qlength, qlength), qlength), h * head_size : (h + 1) * head_size] = (
                    result[h * qlength : (h + 1) * qlength, :]
                )

        scores = jnp.dot(k_ref[...], qt, preferred_element_type=F32) * scale
        weights = jnp.exp2(scores - near_top).astype(BF16)
        mixed = jnp.dot(vt_ref[...], weights, preferred_element_type=F32) + mix_near(near_top)
        store(mixed)
        total = jnp.max(mixed[head_size : head_size + 1])

        @pl.when(jnp.logical_not(total < TOTAL_MAX))
        def _():
            def part(j):
                keys = k_ref[pl.ds(pl.multiple_of(j * chunk, chunk), chunk), :]
                return jnp.dot(keys, qt, preferred_element_type=F32) * scale

            def raise_top(j, top):
                return jnp.maximum(top, jnp.max(part(j), axis=0, keepdims=True))

            top = lax.fori_loop(0, context // chunk, raise_top, near_top)

            def add(j, mixed):
                weights = jnp.exp2(part(j) - top).astype(BF16)
                values = vt_ref[:, pl.ds(pl.multiple_of(j * chunk, chunk), chunk)]
                return mixed + jnp.dot(values, weights, preferred_element_type=F32)

            store(lax.fori_loop(0, context // chunk, add, mix_near(top)))

        return carry

    lax.fori_loop(0, x_ref.shape[0], one, 0)


def attend(table, entry, x, keys, values_t, heads, qlength):
    number, _, head_size = x.shape
    context = keys.shape[1]
    return pl.pallas_call(
        functools.partial(attend_kernel, entry=entry, heads=heads, qlength=qlength, chunk=512),
        in_specs=[SMEM, VMEM, VMEM, VMEM],
        out_specs=VMEM,
        out_shape=jax.ShapeDtypeStruct((number * qlength, heads * head_size), BF16),
        compiler_params=pltpu.CompilerParams(vmem_limit_bytes=20 << 20),
        cost_estimate=pl.CostEstimate(
            flops=8 * number * qlength * heads * context * head_size,
            bytes_accessed=4 << 20,
            transcendentals=number * qlength * heads * context,
        ),
        name="attend",
    )(table, x, keys, values_t)


def project_kernel(a_ref, w_ref, give_ref, keep_ref, *, flip, tile):
    columns = keep_ref.shape[1]
    me = lax.axis_index("tensor")

    def one(i, carry):
        out = pl.ds(pl.multiple_of(i * tile, tile), tile)
        for ref, block in ((give_ref, me ^ flip ^ 1), (keep_ref, me ^ flip)):
            source = pl.ds(pl.multiple_of(block * columns + i * tile, tile), tile)
            product = jnp.dot(a_ref[...], w_ref[:, source], preferred_element_type=F32)
            ref[:, out] = product.astype(ref.dtype)
        return carry

    lax.fori_loop(0, columns // tile, one, 0)


def project(rows, weight, flip, shares, tile):
    number, depth = rows.shape
    columns = weight.shape[1] // shares
    return pl.pallas_call(
        functools.partial(project_kernel, flip=flip, tile=tile),
        in_specs=[VMEM, VMEM],
        out_specs=[VMEM, VMEM],
        out_shape=[
            jax.ShapeDtypeStruct((number, columns), BF16),
            jax.ShapeDtypeStruct((number, columns), F32),
        ],
        compiler_params=pltpu.CompilerParams(vmem_limit_bytes=12 << 20),
        cost_estimate=pl.CostEstimate(
            flops=4 * number * depth * columns, bytes_accessed=4 * depth * columns, transcendentals=0
        ),
        name="project",
    )(rows, weight)


def finish_kernel(table_ref, counts_ref, kept_ref, core_ref, far_ref, *refs, first, qlength):
    o_ref, block_ref, sems = refs[-3:]
    copies = []
    for i in range(block_ref.shape[0]):
        place = jnp.maximum(table_ref[first + i], 0)
        rows = slice(i * qlength, (i + 1) * qlength)
        total = kept_ref[rows, :] + core_ref[rows, :].astype(F32) + far_ref[rows, :].astype(F32)
        t = lax.broadcasted_iota(jnp.int32, total.shape, 0)
        block_ref[i] = jnp.where(t < counts_ref[0, place], total, 0.0).astype(BF16)
        target = o_ref.at[pl.ds(pl.multiple_of(place * qlength, qlength), qlength), :]
        copies.append(pltpu.make_async_copy(block_ref.at[i], target, sems.at[i]))
        copies[-1].start()
    for copy in copies:
        copy.wait()


def finish(table, counts, kept, from_core, from_far, first, previous, rows, qlength):
    number, columns = kept.shape[0] // qlength, kept.shape[1]
    extra = [] if previous is None else [pltpu.with_memory_space_constraint(previous, pltpu.HBM)]
    hbm = pl.BlockSpec(memory_space=pltpu.HBM)
    return pl.pallas_call(
        functools.partial(finish_kernel, first=first, qlength=qlength),
        in_specs=[SMEM, SMEM, VMEM, VMEM, VMEM] + [hbm] * len(extra),
        out_specs=hbm,
        out_shape=pltpu.HBM((rows, columns), BF16),
        scratch_shapes=[pltpu.VMEM((number, qlength, columns), BF16), pltpu.SemaphoreType.DMA((number,))],
        input_output_aliases={5: 0} if extra else {},
        compiler_params=pltpu.CompilerParams(vmem_limit_bytes=16 << 20),
        cost_estimate=pl.CostEstimate(flops=0, bytes_accessed=20 * number * qlength * columns, transcendentals=0),
        name="finish",
    )(table, counts, kept, from_core, from_far, *extra)


def by_shift(shift, replicas):
    return [(i, (i + shift) % replicas) for i in range(replicas)]


def small_slice(groups, replicas, shares):
    return groups <= 2 and replicas == 4 and shares == 4


def project_out(table, counts, results, weight, shares, first, out, rows, qlength):
    other_core = [(i, i ^ 1) for i in range(shares)]
    other_chip = [(i, i ^ 2) for i in range(shares)]
    tile = 512
    far_give, far_keep = project(results, weight, 2, shares, tile)
    far_core = lax.ppermute(far_give, "tensor", other_core)
    near_give, near_keep = project(results, weight, 0, shares, tile)
    near_core = lax.ppermute(near_give, "tensor", other_core)
    chip_sum = (far_keep + far_core.astype(F32)).astype(BF16)
    far = lax.ppermute(chip_sum, "tensor", other_chip)
    return finish(table, counts, near_keep, near_core, far, first, out, rows, qlength)


def answer_by_first_slots(queries, own, keys, values_t, stored, ids, heads, qlength):
    replicas = stored.shape[1]
    route = functools.partial(route_first, replicas)
    table, packed = pack(stored, ids, queries, own, replicas, route)
    arrived = [packed[0]] + [lax.ppermute(packed[s], "replica", by_shift(s, replicas)) for s in range(1, replicas)]
    result = attend(table, replicas * CAP, jnp.concatenate(arrived), keys, values_t, heads, qlength)
    parts = result.reshape(replicas, CAP * qlength, -1)
    returned = [parts[0]] + [lax.ppermute(parts[s], "replica", by_shift(-s, replicas)) for s in range(1, replicas)]
    return table, jnp.concatenate(returned)


def on_device(queries, new_kv, cache_kv, stored, haystack_ids, token_counts, out_weight):
    groups = lax.axis_size("groups")
    replicas = lax.axis_size("replica")
    shares = lax.axis_size("tensor")
    slots, context = cache_kv.shape[:2]
    head_size = cache_kv.shape[-1]
    questions = haystack_ids.shape[0]
    rows = queries.shape[0]
    qlength = rows // questions
    heads = queries.shape[1] // head_size
    own = new_kv.reshape(2 * rows, head_size)
    pairs = cache_kv.reshape(-1, head_size)
    ids = haystack_ids.T
    stored = stored.T

    if small_slice(groups, replicas, shares) and replicas * CAP == questions and slots == 2:
        table, packed = pack(stored, ids, queries, own, 4, route_near)
        arrived, returned = dict(enumerate(packed)), {}
        shifts = {2: 1, 3: -1}
        for s, shift in shifts.items():
            arrived[s] = lax.ppermute(packed[s], "replica", by_shift(shift, replicas))
        for s in range(4):
            if s < 2:
                previous, after = ((keys, values_t), returned[0]) if s else (None, None)
                keys, values_t = split(pairs, context, slots, s, previous, after)
            returned[s] = attend(table, 8 + s, arrived[s], keys, values_t, heads, qlength)
            if s in shifts:
                returned[s] = lax.ppermute(returned[s], "replica", by_shift(-shifts[s], replicas))
        out = None
        for s in range(4):
            out = project_out(table, token_counts, returned[s], out_weight, shares, s * CAP, out, rows, qlength)
        failed = table[12]
        if groups == 2:
            failed = failed + lax.ppermute(failed, "groups", [(0, 1), (1, 0)])

        def again():
            keys, values_t = split(pairs, context, 1)
            table, results = answer_by_first_slots(queries, own, keys, values_t, stored, ids, heads, qlength)
            return project_out(table, token_counts, results, out_weight, shares, 0, None, rows, qlength)

        return lax.cond(failed > 0, again, lambda: out)

    keys, values_t = split(pairs, context, 1)
    table, results = answer_by_first_slots(queries, own, keys, values_t, stored, ids, heads, qlength)
    blocks = results.reshape(replicas * CAP, qlength, -1)
    match = table[None, : replicas * CAP] == jnp.arange(questions, dtype=jnp.int32)[:, None]
    position = jnp.argmax(match.astype(jnp.int32), axis=1)
    used = jnp.arange(qlength, dtype=jnp.int32)[None, :] < token_counts[0][:, None]
    attended = jnp.where(used[..., None], blocks[position], jnp.zeros((), BF16)).reshape(rows, -1)
    summed = lax.psum_scatter(
        lax.dot_general(out_weight, attended, (((0,), (1,)), ((), ())), preferred_element_type=F32),
        "tensor",
        scatter_dimension=0,
        tiled=True,
    )
    return summed.T.astype(BF16)


def solution(mesh):
    in_specs = (
        P(("groups", "replica"), "tensor"),
        P(("groups", "replica"), None, "tensor"),
        P(("groups", "replica"), None, None, "tensor"),
        P("groups", None),
        P(("groups", "replica"), None),
        P(("groups", "replica"), None),
        P("tensor", None),
    )
    out_specs = P(("groups", "replica"), "tensor")
    return jax.shard_map(
        on_device, mesh=mesh, in_specs=in_specs, out_specs=out_specs, check_vma=False
    )
```

```python
import functools
import math

import jax
import jax.numpy as jnp
from jax import lax
from jax.experimental import pallas as pl
from jax.experimental.pallas import tpu as pltpu
from jax.sharding import PartitionSpec as P


CAP = 2
BF16 = jnp.bfloat16
F32 = jnp.float32
LOG2E = 1.4426950408889634
TOTAL_MAX = 1e30
VMEM = pl.BlockSpec(memory_space=pltpu.VMEM)
SMEM = pl.BlockSpec(memory_space=pltpu.SMEM)


def pack_kernel(stored_hbm, ids_hbm, q_hbm, own_hbm, table_ref, failed_ref, *refs, route, heads, qlength):
    number = len(refs) - 5
    out_refs = refs[:number]
    stored_ref, ids_ref, q_ref, own_ref, sems = refs[number:]
    head_size = own_ref.shape[1]
    questions = ids_ref.shape[1]
    pairs = ((stored_hbm, stored_ref), (ids_hbm, ids_ref), (q_hbm, q_ref), (own_hbm, own_ref))
    copies = [pltpu.make_async_copy(source, target, sems.at[i]) for i, (source, target) in enumerate(pairs)]
    for copy in copies:
        copy.start()
    for copy in copies[:2]:
        copy.wait()
    places = []
    for s, haystack in enumerate(route(stored_ref, table_ref, failed_ref)):
        count = jnp.int32(0)
        found = [jnp.int32(-1)] * CAP
        for i in range(questions):
            hit = ids_ref[0, i] == haystack
            for j in range(CAP):
                found[j] = jnp.where(hit & (count == j), jnp.int32(i), found[j])
            count = count + hit.astype(jnp.int32)
        for j in range(CAP):
            table_ref[s * CAP + j] = found[j]
        places.append([jnp.maximum(place, 0) for place in found])
    for copy in copies[2:]:
        copy.wait()
    for s, out_ref in enumerate(out_refs):
        for j, place in enumerate(places[s]):
            rows = q_ref[pl.ds(pl.multiple_of(place * qlength, qlength), qlength), :]
            for h in range(heads):
                out_ref[j, h * qlength : (h + 1) * qlength, :] = rows[:, h * head_size : (h + 1) * head_size]
            own = own_ref[pl.ds(pl.multiple_of(place * 2 * qlength, 2 * qlength), 2 * qlength), :]
            out_ref[j, heads * qlength :, :] = own


def route_first(replicas, stored_ref, table_ref, failed_ref):
    failed_ref[0] = jnp.int32(0)
    me = lax.axis_index("replica")
    return [stored_ref[0, lax.rem(me + s, replicas)] for s in range(replicas)]


def route_near(stored_ref, table_ref, failed_ref):
    me = lax.axis_index("replica")

    def held(replica):
        return [stored_ref[slot, replica] for slot in range(2)]

    def plan(replica):
        here, after, before = [held(lax.rem(replica + d, 4)) for d in (0, 1, 3)]
        done = jnp.bool_(False)
        slots = [jnp.int32(0), jnp.int32(0)]
        chosen = [after[0], before[0]]
        for i in range(2):
            for k in range(2):
                one, two = after[i], before[k]
                fits = (one != here[0]) & (one != here[1]) & (two != here[0]) & (two != here[1]) & (one != two)
                take = fits & jnp.logical_not(done)
                slots = [jnp.where(take, i, slots[0]), jnp.where(take, k, slots[1])]
                chosen = [jnp.where(take, one, chosen[0]), jnp.where(take, two, chosen[1])]
                done = done | fits
        return slots, chosen, done

    plans = [plan(lax.rem(me + d, 4)) for d in range(4)]
    failed = jnp.int32(0)
    for _, _, done in plans:
        failed = jnp.where(done, failed, 1)
    table_ref[10] = plans[3][0][0]
    table_ref[11] = plans[1][0][1]
    failed_ref[0] = failed
    return held(me) + plans[0][1]


def pack(stored, ids, queries, own, phases, route):
    questions = ids.shape[1]
    head_size = own.shape[1]
    qlength = queries.shape[0] // questions
    heads = queries.shape[1] // head_size
    rows = heads * qlength + 2 * qlength
    arguments = [pltpu.with_memory_space_constraint(x, pltpu.HBM) for x in (stored, ids, queries, own)]
    out = pl.pallas_call(
        functools.partial(pack_kernel, route=route, heads=heads, qlength=qlength),
        in_specs=[pl.BlockSpec(memory_space=pltpu.HBM)] * 4,
        out_specs=[SMEM, SMEM] + [VMEM] * phases,
        out_shape=[jax.ShapeDtypeStruct((size,), jnp.int32) for size in (phases * (CAP + 1), 1)]
        + [jax.ShapeDtypeStruct((CAP, rows, head_size), BF16)] * phases,
        scratch_shapes=[
            pltpu.SMEM(stored.shape, jnp.int32),
            pltpu.SMEM(ids.shape, jnp.int32),
            pltpu.VMEM(queries.shape, BF16),
            pltpu.VMEM(own.shape, BF16),
            pltpu.SemaphoreType.DMA((4,)),
        ],
        compiler_params=pltpu.CompilerParams(vmem_limit_bytes=16 << 20),
        cost_estimate=pl.CostEstimate(flops=0, bytes_accessed=4 << 20, transcendentals=0),
        name="pack",
    )(*arguments)
    return out[0], out[1], out[2:]


def split_kernel(x_ref, *refs, slot):
    k_ref, vt_ref, pairs_ref, wide_ref, sems = refs[-5:]
    parts, block, head_size = pairs_ref.shape
    half = block // 2
    depth, context = vt_ref.shape[1:]
    copies = [
        pltpu.make_async_copy(x_ref.at[pl.ds((slot * parts + i) * block, block), :], pairs_ref.at[i], sems.at[i])
        for i in range(parts)
    ]
    for copy in copies:
        copy.start()
    vt_ref[slot, head_size:, :] = jnp.ones((depth - head_size, context), BF16)
    for i, copy in enumerate(copies):
        copy.wait()
        wide = wide_ref.at[i % 2]
        wide[...] = pairs_ref[i].astype(F32)
        k_ref[slot, i * half : (i + 1) * half, :] = wide[pl.ds(0, half, stride=2), :].astype(BF16)
        values = wide[pl.ds(1, half, stride=2), :]
        vt_ref[slot, :head_size, i * half : (i + 1) * half] = values.T.astype(BF16)


def split(pairs, context, slots, slot=0, previous=None, after=None):
    head_size = pairs.shape[1]
    parts = 8
    block = 2 * context // parts
    hbm = pl.BlockSpec(memory_space=pltpu.HBM)
    extra = [] if previous is None else [*previous, after]
    return pl.pallas_call(
        functools.partial(split_kernel, slot=slot),
        in_specs=[hbm] + ([VMEM, VMEM, pl.BlockSpec(memory_space=pl.ANY)] if extra else []),
        out_specs=[VMEM, VMEM],
        out_shape=[
            jax.ShapeDtypeStruct((slots, context, head_size), BF16),
            jax.ShapeDtypeStruct((slots, head_size + 16, context), BF16),
        ],
        scratch_shapes=[
            pltpu.VMEM((parts, block, head_size), BF16),
            pltpu.VMEM((2, block, head_size), F32),
            pltpu.SemaphoreType.DMA((parts,)),
        ],
        input_output_aliases={1: 0, 2: 1} if extra else {},
        compiler_params=pltpu.CompilerParams(vmem_limit_bytes=16 << 20),
        cost_estimate=pl.CostEstimate(flops=0, bytes_accessed=8 * context * head_size, transcendentals=0),
        name="split",
    )(pltpu.with_memory_space_constraint(pairs, pltpu.HBM), *extra)


def attend_kernel(table_ref, x_ref, keys_ref, values_ref, o_ref, *, entry, heads, qlength, chunk):
    slot = entry if isinstance(entry, int) else table_ref[entry[0]]
    k_ref, vt_ref = keys_ref.at[slot], values_ref.at[slot]
    context, head_size = k_ref.shape
    scale = LOG2E / math.sqrt(head_size)
    rows = heads * qlength

    def one(i, carry):
        qt = x_ref[i, :rows, :].T
        own = x_ref[i, rows:, :]
        near = jnp.dot(own, qt, preferred_element_type=F32) * scale
        u2 = lax.broadcasted_iota(jnp.int32, near.shape, 0)
        t = lax.broadcasted_iota(jnp.int32, near.shape, 1) % qlength
        near = jnp.where((u2 % 2 == 0) & (u2 <= 2 * t), near, -jnp.inf)
        near_top = jnp.max(near, axis=0, keepdims=True)
        own_t = own.astype(F32).T.astype(BF16)
        own_vt = jnp.concatenate([own_t, jnp.ones((16, own.shape[0]), BF16)], axis=0)

        def mix_near(top):
            weights = pltpu.roll(jnp.exp2(near - top), 1, 0).astype(BF16)
            return jnp.dot(own_vt, weights, preferred_element_type=F32)

        def store(mixed):
            result = (mixed[:head_size] / mixed[head_size : head_size + 1]).T.astype(BF16)
            for h in range(heads):
                o_ref[pl.ds(pl.multiple_of(i * qlength, qlength), qlength), h * head_size : (h + 1) * head_size] = (
                    result[h * qlength : (h + 1) * qlength, :]
                )

        scores = jnp.dot(k_ref[...], qt, preferred_element_type=F32) * scale
        weights = jnp.exp2(scores - near_top).astype(BF16)
        mixed = jnp.dot(vt_ref[...], weights, preferred_element_type=F32) + mix_near(near_top)
        store(mixed)
        total = jnp.max(mixed[head_size : head_size + 1])

        @pl.when(jnp.logical_not(total < TOTAL_MAX))
        def _():
            def part(j):
                keys = k_ref[pl.ds(pl.multiple_of(j * chunk, chunk), chunk), :]
                return jnp.dot(keys, qt, preferred_element_type=F32) * scale

            def raise_top(j, top):
                return jnp.maximum(top, jnp.max(part(j), axis=0, keepdims=True))

            top = lax.fori_loop(0, context // chunk, raise_top, near_top)

            def add(j, mixed):
                weights = jnp.exp2(part(j) - top).astype(BF16)
                values = vt_ref[:, pl.ds(pl.multiple_of(j * chunk, chunk), chunk)]
                return mixed + jnp.dot(values, weights, preferred_element_type=F32)

            store(lax.fori_loop(0, context // chunk, add, mix_near(top)))

        return carry

    lax.fori_loop(0, x_ref.shape[0], one, 0)


def attend(table, entry, x, keys, values_t, heads, qlength):
    number, _, head_size = x.shape
    context = keys.shape[1]
    return pl.pallas_call(
        functools.partial(attend_kernel, entry=entry, heads=heads, qlength=qlength, chunk=512),
        in_specs=[SMEM, VMEM, VMEM, VMEM],
        out_specs=VMEM,
        out_shape=jax.ShapeDtypeStruct((number * qlength, heads * head_size), BF16),
        compiler_params=pltpu.CompilerParams(vmem_limit_bytes=20 << 20),
        cost_estimate=pl.CostEstimate(
            flops=8 * number * qlength * heads * context * head_size,
            bytes_accessed=4 << 20,
            transcendentals=number * qlength * heads * context,
        ),
        name="attend",
    )(table, x, keys, values_t)


def project_kernel(a_ref, w_ref, *out_refs, flips, tile):
    columns = out_refs[0].shape[1]
    me = lax.axis_index("tensor")

    def one(i, carry):
        out = pl.ds(pl.multiple_of(i * tile, tile), tile)
        for ref, flip in zip(out_refs, flips):
            source = pl.ds(pl.multiple_of((me ^ flip) * columns + i * tile, tile), tile)
            product = jnp.dot(a_ref[...], w_ref[:, source], preferred_element_type=F32)
            ref[:, out] = product.astype(ref.dtype)
        return carry

    lax.fori_loop(0, columns // tile, one, 0)


def project(rows, weight, shares, tile, flips, types):
    number, depth = rows.shape
    columns = weight.shape[1] // shares
    return pl.pallas_call(
        functools.partial(project_kernel, flips=flips, tile=tile),
        in_specs=[VMEM, VMEM],
        out_specs=[VMEM] * len(flips),
        out_shape=[jax.ShapeDtypeStruct((number, columns), kind) for kind in types],
        compiler_params=pltpu.CompilerParams(vmem_limit_bytes=12 << 20),
        cost_estimate=pl.CostEstimate(
            flops=2 * len(flips) * number * depth * columns,
            bytes_accessed=2 * len(flips) * depth * columns,
            transcendentals=0,
        ),
        name="project",
    )(rows, weight)


def finish_kernel(table_ref, counts_ref, a_ref, w_ref, core_ref, far_ref, *refs, first, qlength, tile):
    o_ref, block_ref, sems = refs[-3:]
    number, _, columns = block_ref.shape
    me = lax.axis_index("tensor")
    places = [jnp.maximum(table_ref[first + i], 0) for i in range(number)]
    counts = [counts_ref[0, place] for place in places]
    t = lax.broadcasted_iota(jnp.int32, (qlength, tile), 0)

    def one(j, carry):
        out = pl.ds(pl.multiple_of(j * tile, tile), tile)
        source = pl.ds(pl.multiple_of(me * columns + j * tile, tile), tile)
        total = jnp.dot(a_ref[...], w_ref[:, source], preferred_element_type=F32)
        total = total + core_ref[:, out].astype(F32) + far_ref[:, out].astype(F32)
        for i in range(number):
            block = total[i * qlength : (i + 1) * qlength, :]
            block_ref[i, :, out] = jnp.where(t < counts[i], block, 0.0).astype(BF16)
        return carry

    lax.fori_loop(0, columns // tile, one, 0)
    copies = []
    for i, place in enumerate(places):
        target = o_ref.at[pl.ds(pl.multiple_of(place * qlength, qlength), qlength), :]
        copies.append(pltpu.make_async_copy(block_ref.at[i], target, sems.at[i]))
        copies[-1].start()
    for copy in copies:
        copy.wait()


def finish(table, counts, results, weight, from_core, from_far, first, previous, rows, qlength, tile):
    number, columns = results.shape[0] // qlength, from_far.shape[1]
    extra = [] if previous is None else [pltpu.with_memory_space_constraint(previous, pltpu.HBM)]
    hbm = pl.BlockSpec(memory_space=pltpu.HBM)
    return pl.pallas_call(
        functools.partial(finish_kernel, first=first, qlength=qlength, tile=tile),
        in_specs=[SMEM, SMEM, VMEM, VMEM, VMEM, VMEM] + [hbm] * len(extra),
        out_specs=hbm,
        out_shape=pltpu.HBM((rows, columns), BF16),
        scratch_shapes=[pltpu.VMEM((number, qlength, columns), BF16), pltpu.SemaphoreType.DMA((number,))],
        input_output_aliases={6: 0} if extra else {},
        compiler_params=pltpu.CompilerParams(vmem_limit_bytes=12 << 20),
        cost_estimate=pl.CostEstimate(
            flops=2 * results.shape[0] * results.shape[1] * columns,
            bytes_accessed=2 * results.shape[1] * columns,
            transcendentals=0,
        ),
        name="finish",
    )(table, counts, results, weight, from_core, from_far, *extra)


def by_shift(shift, replicas):
    return [(i, (i + shift) % replicas) for i in range(replicas)]


def small_slice(groups, replicas, shares):
    return groups <= 2 and replicas == 4 and shares == 4


def project_out(table, counts, results, weight, shares, first, out, rows, qlength):
    other_core = [(i, i ^ 1) for i in range(shares)]
    other_chip = [(i, i ^ 2) for i in range(shares)]
    tile = 512
    far_give, far_keep = project(results, weight, shares, tile, (3, 2), (BF16, F32))
    far_core = lax.ppermute(far_give, "tensor", other_core)
    (near_give,) = project(results, weight, shares, tile, (1,), (BF16,))
    near_core = lax.ppermute(near_give, "tensor", other_core)
    chip_sum = (far_keep + far_core.astype(F32)).astype(BF16)
    far = lax.ppermute(chip_sum, "tensor", other_chip)
    return finish(table, counts, results, weight, near_core, far, first, out, rows, qlength, tile)


def answer_by_first_slots(queries, own, keys, values_t, stored, ids, heads, qlength):
    replicas = stored.shape[1]
    route = functools.partial(route_first, replicas)
    table, _, packed = pack(stored, ids, queries, own, replicas, route)
    arrived = [packed[0]] + [lax.ppermute(packed[s], "replica", by_shift(s, replicas)) for s in range(1, replicas)]
    result = attend(table, 0, jnp.concatenate(arrived), keys, values_t, heads, qlength)
    parts = result.reshape(replicas, CAP * qlength, -1)
    returned = [parts[0]] + [lax.ppermute(parts[s], "replica", by_shift(-s, replicas)) for s in range(1, replicas)]
    return table, jnp.concatenate(returned)


def on_device(queries, new_kv, cache_kv, stored, haystack_ids, token_counts, out_weight):
    groups = lax.axis_size("groups")
    replicas = lax.axis_size("replica")
    shares = lax.axis_size("tensor")
    slots, context = cache_kv.shape[:2]
    head_size = cache_kv.shape[-1]
    questions = haystack_ids.shape[0]
    rows = queries.shape[0]
    qlength = rows // questions
    heads = queries.shape[1] // head_size
    own = new_kv.reshape(2 * rows, head_size)
    pairs = cache_kv.reshape(-1, head_size)
    ids = haystack_ids.T
    stored = stored.T

    if small_slice(groups, replicas, shares) and replicas * CAP == questions and slots == 2:
        table, failed, packed = pack(stored, ids, queries, own, 4, route_near)
        arrived, returned = dict(enumerate(packed)), {}
        shifts = {2: 1, 3: -1}
        for s, shift in shifts.items():
            arrived[s] = lax.ppermute(packed[s], "replica", by_shift(shift, replicas))
        for s in range(4):
            if s < 2:
                previous, after = ((keys, values_t), returned[0]) if s else (None, None)
                keys, values_t = split(pairs, context, slots, s, previous, after)
            returned[s] = attend(table, s if s < 2 else (8 + s,), arrived[s], keys, values_t, heads, qlength)
            if s in shifts:
                returned[s] = lax.ppermute(returned[s], "replica", by_shift(-shifts[s], replicas))
        out = None
        for s in range(4):
            out = project_out(table, token_counts, returned[s], out_weight, shares, s * CAP, out, rows, qlength)

        def again():
            keys, values_t = split(pairs, context, 1)
            table, results = answer_by_first_slots(queries, own, keys, values_t, stored, ids, heads, qlength)
            return project_out(table, token_counts, results, out_weight, shares, 0, None, rows, qlength)

        return lax.cond(failed[0] > 0, again, lambda: out)

    keys, values_t = split(pairs, context, 1)
    table, results = answer_by_first_slots(queries, own, keys, values_t, stored, ids, heads, qlength)
    blocks = results.reshape(replicas * CAP, qlength, -1)
    match = table[None, : replicas * CAP] == jnp.arange(questions, dtype=jnp.int32)[:, None]
    position = jnp.argmax(match.astype(jnp.int32), axis=1)
    used = jnp.arange(qlength, dtype=jnp.int32)[None, :] < token_counts[0][:, None]
    attended = jnp.where(used[..., None], blocks[position], jnp.zeros((), BF16)).reshape(rows, -1)
    summed = lax.psum_scatter(
        lax.dot_general(out_weight, attended, (((0,), (1,)), ((), ())), preferred_element_type=F32),
        "tensor",
        scatter_dimension=0,
        tiled=True,
    )
    return summed.T.astype(BF16)


def solution(mesh):
    in_specs = (
        P(("groups", "replica"), "tensor"),
        P(("groups", "replica"), None, "tensor"),
        P(("groups", "replica"), None, None, "tensor"),
        P("groups", None),
        P(("groups", "replica"), None),
        P(("groups", "replica"), None),
        P("tensor", None),
    )
    out_specs = P(("groups", "replica"), "tensor")
    return jax.shard_map(
        on_device, mesh=mesh, in_specs=in_specs, out_specs=out_specs, check_vma=False
    )
```

```python
import functools
import math

import jax
import jax.numpy as jnp
from jax import lax
from jax.experimental import pallas as pl
from jax.experimental.pallas import tpu as pltpu
from jax.sharding import PartitionSpec as P


CAP = 2
BF16 = jnp.bfloat16
F32 = jnp.float32
LOG2E = 1.4426950408889634
TOTAL_MAX = 1e30
VMEM = pl.BlockSpec(memory_space=pltpu.VMEM)
SMEM = pl.BlockSpec(memory_space=pltpu.SMEM)


def pack_kernel(stored_hbm, ids_hbm, q_hbm, own_hbm, kv_hbm, table_ref, failed_ref, *refs, route, heads, qlength):
    number = len(refs) - 10
    out_refs, (k_ref, vt_ref) = refs[:number], refs[number : number + 2]
    stored_ref, ids_ref, q_ref, own_ref, sems, pairs_ref, wide_ref, kv_sems = refs[number + 2 :]
    head_size = own_ref.shape[1]
    questions = ids_ref.shape[1]
    pairs = ((stored_hbm, stored_ref), (ids_hbm, ids_ref), (q_hbm, q_ref), (own_hbm, own_ref))
    copies = [pltpu.make_async_copy(source, target, sems.at[i]) for i, (source, target) in enumerate(pairs)]
    kv_copies = split_copies(kv_hbm, pairs_ref, kv_sems, 0)
    for copy in copies + kv_copies:
        copy.start()
    for copy in copies[:2]:
        copy.wait()
    places = []
    for s, haystack in enumerate(route(stored_ref, table_ref, failed_ref)):
        count = jnp.int32(0)
        found = [jnp.int32(-1)] * CAP
        for i in range(questions):
            hit = ids_ref[0, i] == haystack
            for j in range(CAP):
                found[j] = jnp.where(hit & (count == j), jnp.int32(i), found[j])
            count = count + hit.astype(jnp.int32)
        for j in range(CAP):
            table_ref[s * CAP + j] = found[j]
        places.append([jnp.maximum(place, 0) for place in found])
    for copy in copies[2:]:
        copy.wait()
    for s, out_ref in enumerate(out_refs):
        for j, place in enumerate(places[s]):
            rows = q_ref[pl.ds(pl.multiple_of(place * qlength, qlength), qlength), :]
            for h in range(heads):
                out_ref[j, h * qlength : (h + 1) * qlength, :] = rows[:, h * head_size : (h + 1) * head_size]
            own = own_ref[pl.ds(pl.multiple_of(place * 2 * qlength, 2 * qlength), 2 * qlength), :]
            out_ref[j, heads * qlength :, :] = own
    split_arrived(kv_copies, k_ref, vt_ref, pairs_ref, wide_ref, 0)


def route_first(replicas, stored_ref, table_ref, failed_ref):
    failed_ref[0] = jnp.int32(0)
    me = lax.axis_index("replica")
    return [stored_ref[0, lax.rem(me + s, replicas)] for s in range(replicas)]


def route_near(stored_ref, table_ref, failed_ref):
    me = lax.axis_index("replica")

    def held(replica):
        return [stored_ref[slot, replica] for slot in range(2)]

    def plan(replica):
        here, after, before = [held(lax.rem(replica + d, 4)) for d in (0, 1, 3)]
        done = jnp.bool_(False)
        slots = [jnp.int32(0), jnp.int32(0)]
        chosen = [after[0], before[0]]
        for i in range(2):
            for k in range(2):
                one, two = after[i], before[k]
                fits = (one != here[0]) & (one != here[1]) & (two != here[0]) & (two != here[1]) & (one != two)
                take = fits & jnp.logical_not(done)
                slots = [jnp.where(take, i, slots[0]), jnp.where(take, k, slots[1])]
                chosen = [jnp.where(take, one, chosen[0]), jnp.where(take, two, chosen[1])]
                done = done | fits
        return slots, chosen, done

    plans = [plan(lax.rem(me + d, 4)) for d in range(4)]
    failed = jnp.int32(0)
    for _, _, done in plans:
        failed = jnp.where(done, failed, 1)
    table_ref[10] = plans[3][0][0]
    table_ref[11] = plans[1][0][1]
    failed_ref[0] = failed
    return held(me) + plans[0][1]


def pack(stored, ids, queries, own, pairs, context, slots, phases, route):
    questions = ids.shape[1]
    head_size = own.shape[1]
    qlength = queries.shape[0] // questions
    heads = queries.shape[1] // head_size
    rows = heads * qlength + 2 * qlength
    arguments = [pltpu.with_memory_space_constraint(x, pltpu.HBM) for x in (stored, ids, queries, own, pairs)]
    split_out, split_scratch = split_shapes(context, head_size, slots)
    out = pl.pallas_call(
        functools.partial(pack_kernel, route=route, heads=heads, qlength=qlength),
        in_specs=[pl.BlockSpec(memory_space=pltpu.HBM)] * 5,
        out_specs=[SMEM, SMEM] + [VMEM] * (phases + 2),
        out_shape=[jax.ShapeDtypeStruct((size,), jnp.int32) for size in (phases * (CAP + 1), 1)]
        + [jax.ShapeDtypeStruct((CAP, rows, head_size), BF16)] * phases
        + split_out,
        scratch_shapes=[
            pltpu.SMEM(stored.shape, jnp.int32),
            pltpu.SMEM(ids.shape, jnp.int32),
            pltpu.VMEM(queries.shape, BF16),
            pltpu.VMEM(own.shape, BF16),
            pltpu.SemaphoreType.DMA((4,)),
            *split_scratch,
        ],
        compiler_params=pltpu.CompilerParams(vmem_limit_bytes=16 << 20),
        cost_estimate=pl.CostEstimate(flops=0, bytes_accessed=4 << 20, transcendentals=0),
        name="pack",
    )(*arguments)
    return out[0], out[1], out[2:-2], out[-2:]


def split_copies(x_ref, pairs_ref, sems, slot):
    parts, block, _ = pairs_ref.shape
    return [
        pltpu.make_async_copy(x_ref.at[pl.ds((slot * parts + i) * block, block), :], pairs_ref.at[i], sems.at[i])
        for i in range(parts)
    ]


def split_arrived(copies, k_ref, vt_ref, pairs_ref, wide_ref, slot):
    half, head_size = pairs_ref.shape[1] // 2, pairs_ref.shape[2]
    depth, context = vt_ref.shape[1:]
    vt_ref[slot, head_size:, :] = jnp.ones((depth - head_size, context), BF16)
    for i, copy in enumerate(copies):
        copy.wait()
        wide = wide_ref.at[i % 2]
        wide[...] = pairs_ref[i].astype(F32)
        k_ref[slot, i * half : (i + 1) * half, :] = wide[pl.ds(0, half, stride=2), :].astype(BF16)
        values = wide[pl.ds(1, half, stride=2), :]
        vt_ref[slot, :head_size, i * half : (i + 1) * half] = values.T.astype(BF16)


def split_shapes(context, head_size, slots):
    parts = 8
    block = 2 * context // parts
    out_shape = [
        jax.ShapeDtypeStruct((slots, context, head_size), BF16),
        jax.ShapeDtypeStruct((slots, head_size + 16, context), BF16),
    ]
    scratch_shapes = [
        pltpu.VMEM((parts, block, head_size), BF16),
        pltpu.VMEM((2, block, head_size), F32),
        pltpu.SemaphoreType.DMA((parts,)),
    ]
    return out_shape, scratch_shapes


def split_kernel(x_ref, keys_ref, values_ref, after_ref, k_ref, vt_ref, pairs_ref, wide_ref, sems, *, slot):
    copies = split_copies(x_ref, pairs_ref, sems, slot)
    for copy in copies:
        copy.start()
    split_arrived(copies, k_ref, vt_ref, pairs_ref, wide_ref, slot)


def split(pairs, keys, values_t, slot, after):
    slots, context, head_size = keys.shape
    out_shape, scratch_shapes = split_shapes(context, head_size, slots)
    hbm = pl.BlockSpec(memory_space=pltpu.HBM)
    return pl.pallas_call(
        functools.partial(split_kernel, slot=slot),
        in_specs=[hbm, VMEM, VMEM, pl.BlockSpec(memory_space=pl.ANY)],
        out_specs=[VMEM, VMEM],
        out_shape=out_shape,
        scratch_shapes=scratch_shapes,
        input_output_aliases={1: 0, 2: 1},
        compiler_params=pltpu.CompilerParams(vmem_limit_bytes=16 << 20),
        cost_estimate=pl.CostEstimate(flops=0, bytes_accessed=8 * context * head_size, transcendentals=0),
        name="split",
    )(pltpu.with_memory_space_constraint(pairs, pltpu.HBM), keys, values_t, after)


def attend_kernel(table_ref, x_ref, keys_ref, values_ref, o_ref, *, entry, heads, qlength, chunk):
    slot = entry if isinstance(entry, int) else table_ref[entry[0]]
    k_ref, vt_ref = keys_ref.at[slot], values_ref.at[slot]
    context, head_size = k_ref.shape
    scale = LOG2E / math.sqrt(head_size)
    rows = heads * qlength

    def one(i, carry):
        qt = x_ref[i, :rows, :].T
        own = x_ref[i, rows:, :]
        near = jnp.dot(own, qt, preferred_element_type=F32) * scale
        u2 = lax.broadcasted_iota(jnp.int32, near.shape, 0)
        t = lax.broadcasted_iota(jnp.int32, near.shape, 1) % qlength
        near = jnp.where((u2 % 2 == 0) & (u2 <= 2 * t), near, -jnp.inf)
        near_top = jnp.max(near, axis=0, keepdims=True)
        own_t = own.astype(F32).T.astype(BF16)
        own_vt = jnp.concatenate([own_t, jnp.ones((16, own.shape[0]), BF16)], axis=0)

        def mix_near(top):
            weights = pltpu.roll(jnp.exp2(near - top), 1, 0).astype(BF16)
            return jnp.dot(own_vt, weights, preferred_element_type=F32)

        def store(mixed):
            result = (mixed[:head_size] / mixed[head_size : head_size + 1]).T.astype(BF16)
            for h in range(heads):
                o_ref[pl.ds(pl.multiple_of(i * qlength, qlength), qlength), h * head_size : (h + 1) * head_size] = (
                    result[h * qlength : (h + 1) * qlength, :]
                )

        scores = jnp.dot(k_ref[...], qt, preferred_element_type=F32) * scale
        weights = jnp.exp2(scores - near_top).astype(BF16)
        mixed = jnp.dot(vt_ref[...], weights, preferred_element_type=F32) + mix_near(near_top)
        store(mixed)
        total = jnp.max(mixed[head_size : head_size + 1])

        @pl.when(jnp.logical_not(total < TOTAL_MAX))
        def _():
            def part(j):
                keys = k_ref[pl.ds(pl.multiple_of(j * chunk, chunk), chunk), :]
                return jnp.dot(keys, qt, preferred_element_type=F32) * scale

            def raise_top(j, top):
                return jnp.maximum(top, jnp.max(part(j), axis=0, keepdims=True))

            top = lax.fori_loop(0, context // chunk, raise_top, near_top)

            def add(j, mixed):
                weights = jnp.exp2(part(j) - top).astype(BF16)
                values = vt_ref[:, pl.ds(pl.multiple_of(j * chunk, chunk), chunk)]
                return mixed + jnp.dot(values, weights, preferred_element_type=F32)

            store(lax.fori_loop(0, context // chunk, add, mix_near(top)))

        return carry

    lax.fori_loop(0, x_ref.shape[0], one, 0, unroll=x_ref.shape[0] == CAP)


def attend(table, entry, x, keys, values_t, heads, qlength):
    number, _, head_size = x.shape
    context = keys.shape[1]
    return pl.pallas_call(
        functools.partial(attend_kernel, entry=entry, heads=heads, qlength=qlength, chunk=512),
        in_specs=[SMEM, VMEM, VMEM, VMEM],
        out_specs=VMEM,
        out_shape=jax.ShapeDtypeStruct((number * qlength, heads * head_size), BF16),
        compiler_params=pltpu.CompilerParams(vmem_limit_bytes=20 << 20),
        cost_estimate=pl.CostEstimate(
            flops=8 * number * qlength * heads * context * head_size,
            bytes_accessed=4 << 20,
            transcendentals=number * qlength * heads * context,
        ),
        name="attend",
    )(table, x, keys, values_t)


def project_kernel(a_ref, w_ref, *out_refs, flips, tile):
    columns = out_refs[0].shape[1]
    me = lax.axis_index("tensor")

    def one(i, carry):
        out = pl.ds(pl.multiple_of(i * tile, tile), tile)
        for ref, flip in zip(out_refs, flips):
            source = pl.ds(pl.multiple_of((me ^ flip) * columns + i * tile, tile), tile)
            product = jnp.dot(a_ref[...], w_ref[:, source], preferred_element_type=F32)
            ref[:, out] = product.astype(ref.dtype)
        return carry

    lax.fori_loop(0, columns // tile, one, 0)


def project(rows, weight, shares, tile, flips, types):
    number, depth = rows.shape
    columns = weight.shape[1] // shares
    return pl.pallas_call(
        functools.partial(project_kernel, flips=flips, tile=tile),
        in_specs=[VMEM, VMEM],
        out_specs=[VMEM] * len(flips),
        out_shape=[jax.ShapeDtypeStruct((number, columns), kind) for kind in types],
        compiler_params=pltpu.CompilerParams(vmem_limit_bytes=12 << 20),
        cost_estimate=pl.CostEstimate(
            flops=2 * len(flips) * number * depth * columns,
            bytes_accessed=2 * len(flips) * depth * columns,
            transcendentals=0,
        ),
        name="project",
    )(rows, weight)


def finish_kernel(table_ref, counts_ref, kept_ref, core_ref, far_ref, *refs, first, qlength, tile):
    o_ref, block_ref, sems = refs[-3:]
    number, _, columns = block_ref.shape
    places = [jnp.maximum(table_ref[first + i], 0) for i in range(number)]
    counts = [counts_ref[0, place] for place in places]
    t = lax.broadcasted_iota(jnp.int32, (qlength, tile), 0)

    def one(j, carry):
        out = pl.ds(pl.multiple_of(j * tile, tile), tile)
        total = kept_ref[:, out] + core_ref[:, out].astype(F32) + far_ref[:, out].astype(F32)
        for i in range(number):
            block = total[i * qlength : (i + 1) * qlength, :]
            block_ref[i, :, out] = jnp.where(t < counts[i], block, 0.0).astype(BF16)
        return carry

    lax.fori_loop(0, columns // tile, one, 0)
    copies = []
    for i, place in enumerate(places):
        target = o_ref.at[pl.ds(pl.multiple_of(place * qlength, qlength), qlength), :]
        copies.append(pltpu.make_async_copy(block_ref.at[i], target, sems.at[i]))
        copies[-1].start()
    for copy in copies:
        copy.wait()


def finish(table, counts, kept, from_core, from_far, first, previous, rows, qlength, tile):
    number, columns = kept.shape[0] // qlength, kept.shape[1]
    extra = [] if previous is None else [pltpu.with_memory_space_constraint(previous, pltpu.HBM)]
    hbm = pl.BlockSpec(memory_space=pltpu.HBM)
    return pl.pallas_call(
        functools.partial(finish_kernel, first=first, qlength=qlength, tile=tile),
        in_specs=[SMEM, SMEM, VMEM, VMEM, VMEM] + [hbm] * len(extra),
        out_specs=hbm,
        out_shape=pltpu.HBM((rows, columns), BF16),
        scratch_shapes=[pltpu.VMEM((number, qlength, columns), BF16), pltpu.SemaphoreType.DMA((number,))],
        input_output_aliases={5: 0} if extra else {},
        compiler_params=pltpu.CompilerParams(vmem_limit_bytes=12 << 20),
        cost_estimate=pl.CostEstimate(flops=0, bytes_accessed=10 * kept.shape[0] * columns, transcendentals=0),
        name="finish",
    )(table, counts, kept, from_core, from_far, *extra)


def by_shift(shift, replicas):
    return [(i, (i + shift) % replicas) for i in range(replicas)]


def small_slice(groups, replicas, shares):
    return groups <= 2 and replicas == 4 and shares == 4


def project_out(table, counts, results, weight, shares, first, out, rows, qlength):
    other_core = [(i, i ^ 1) for i in range(shares)]
    other_chip = [(i, i ^ 2) for i in range(shares)]
    tile = 512
    far_give, far_keep = project(results, weight, shares, tile, (3, 2), (BF16, F32))
    far_core = lax.ppermute(far_give, "tensor", other_core)
    (near_give,) = project(results, weight, shares, tile, (1,), (BF16,))
    near_core = lax.ppermute(near_give, "tensor", other_core)
    chip_sum = (far_keep + far_core.astype(F32)).astype(BF16)
    far = lax.ppermute(chip_sum, "tensor", other_chip)
    (near_keep,) = project(results, weight, shares, tile, (0,), (F32,))
    return finish(table, counts, near_keep, near_core, far, first, out, rows, qlength, tile)


def answer_by_first_slots(queries, own, pairs, context, stored, ids, heads, qlength):
    replicas = stored.shape[1]
    route = functools.partial(route_first, replicas)
    table, _, packed, (keys, values_t) = pack(stored, ids, queries, own, pairs, context, 1, replicas, route)
    arrived = [packed[0]] + [lax.ppermute(packed[s], "replica", by_shift(s, replicas)) for s in range(1, replicas)]
    result = attend(table, 0, jnp.concatenate(arrived), keys, values_t, heads, qlength)
    parts = result.reshape(replicas, CAP * qlength, -1)
    returned = [parts[0]] + [lax.ppermute(parts[s], "replica", by_shift(-s, replicas)) for s in range(1, replicas)]
    return table, jnp.concatenate(returned)


def on_device(queries, new_kv, cache_kv, stored, haystack_ids, token_counts, out_weight):
    groups = lax.axis_size("groups")
    replicas = lax.axis_size("replica")
    shares = lax.axis_size("tensor")
    slots, context = cache_kv.shape[:2]
    head_size = cache_kv.shape[-1]
    questions = haystack_ids.shape[0]
    rows = queries.shape[0]
    qlength = rows // questions
    heads = queries.shape[1] // head_size
    own = new_kv.reshape(2 * rows, head_size)
    pairs = cache_kv.reshape(-1, head_size)
    ids = haystack_ids.T
    stored = stored.T

    if small_slice(groups, replicas, shares) and replicas * CAP == questions and slots == 2:
        table, failed, packed, (keys, values_t) = pack(
            stored, ids, queries, own, pairs, context, slots, 4, route_near
        )
        arrived, returned = dict(enumerate(packed)), {}
        shifts = {2: 1, 3: -1}
        for s, shift in shifts.items():
            arrived[s] = lax.ppermute(packed[s], "replica", by_shift(shift, replicas))
        for s in range(4):
            if s == 1:
                keys, values_t = split(pairs, keys, values_t, 1, returned[0])
            returned[s] = attend(table, s if s < 2 else (8 + s,), arrived[s], keys, values_t, heads, qlength)
            if s in shifts:
                returned[s] = lax.ppermute(returned[s], "replica", by_shift(-shifts[s], replicas))
        out = None
        for s in range(4):
            out = project_out(table, token_counts, returned[s], out_weight, shares, s * CAP, out, rows, qlength)

        def again():
            table, results = answer_by_first_slots(queries, own, pairs, context, stored, ids, heads, qlength)
            return project_out(table, token_counts, results, out_weight, shares, 0, None, rows, qlength)

        return lax.cond(failed[0] > 0, again, lambda: out)

    table, results = answer_by_first_slots(queries, own, pairs, context, stored, ids, heads, qlength)
    blocks = results.reshape(replicas * CAP, qlength, -1)
    match = table[None, : replicas * CAP] == jnp.arange(questions, dtype=jnp.int32)[:, None]
    position = jnp.argmax(match.astype(jnp.int32), axis=1)
    used = jnp.arange(qlength, dtype=jnp.int32)[None, :] < token_counts[0][:, None]
    attended = jnp.where(used[..., None], blocks[position], jnp.zeros((), BF16)).reshape(rows, -1)
    summed = lax.psum_scatter(
        lax.dot_general(out_weight, attended, (((0,), (1,)), ((), ())), preferred_element_type=F32),
        "tensor",
        scatter_dimension=0,
        tiled=True,
    )
    return summed.T.astype(BF16)


def solution(mesh):
    in_specs = (
        P(("groups", "replica"), "tensor"),
        P(("groups", "replica"), None, "tensor"),
        P(("groups", "replica"), None, None, "tensor"),
        P("groups", None),
        P(("groups", "replica"), None),
        P(("groups", "replica"), None),
        P("tensor", None),
    )
    out_specs = P(("groups", "replica"), "tensor")
    return jax.shard_map(
        on_device, mesh=mesh, in_specs=in_specs, out_specs=out_specs, check_vma=False
    )
```

```python
import functools
import math

import jax
import jax.numpy as jnp
from jax import lax
from jax.experimental import pallas as pl
from jax.experimental.pallas import tpu as pltpu
from jax.sharding import PartitionSpec as P


CAP = 2
BF16 = jnp.bfloat16
F32 = jnp.float32
LOG2E = 1.4426950408889634
TOTAL_MAX = 1e30
VMEM = pl.BlockSpec(memory_space=pltpu.VMEM)
SMEM = pl.BlockSpec(memory_space=pltpu.SMEM)


def pack_kernel(stored_hbm, ids_hbm, q_hbm, own_hbm, kv_hbm, table_ref, failed_ref, *refs, route, heads, qlength):
    number = len(refs) - 10
    out_refs, (k_ref, vt_ref) = refs[:number], refs[number : number + 2]
    stored_ref, ids_ref, q_ref, own_ref, sems, pairs_ref, wide_ref, kv_sems = refs[number + 2 :]
    head_size = own_ref.shape[1]
    questions = ids_ref.shape[1]
    pairs = ((stored_hbm, stored_ref), (ids_hbm, ids_ref), (q_hbm, q_ref), (own_hbm, own_ref))
    copies = [pltpu.make_async_copy(source, target, sems.at[i]) for i, (source, target) in enumerate(pairs)]
    kv_copies = split_copies(kv_hbm, pairs_ref, kv_sems, 0)
    for copy in copies + kv_copies:
        copy.start()
    for copy in copies[:2]:
        copy.wait()
    places = []
    for s, haystack in enumerate(route(stored_ref, table_ref, failed_ref)):
        count = jnp.int32(0)
        found = [jnp.int32(-1)] * CAP
        for i in range(questions):
            hit = ids_ref[0, i] == haystack
            for j in range(CAP):
                found[j] = jnp.where(hit & (count == j), jnp.int32(i), found[j])
            count = count + hit.astype(jnp.int32)
        for j in range(CAP):
            table_ref[s * CAP + j] = found[j]
        places.append([jnp.maximum(place, 0) for place in found])
    for copy in copies[2:]:
        copy.wait()
    for s, out_ref in enumerate(out_refs):
        for j, place in enumerate(places[s]):
            rows = q_ref[pl.ds(pl.multiple_of(place * qlength, qlength), qlength), :]
            for h in range(heads):
                out_ref[j, h * qlength : (h + 1) * qlength, :] = rows[:, h * head_size : (h + 1) * head_size]
            own = own_ref[pl.ds(pl.multiple_of(place * 2 * qlength, 2 * qlength), 2 * qlength), :]
            out_ref[j, heads * qlength :, :] = own
    split_arrived(kv_copies, k_ref, vt_ref, pairs_ref, wide_ref, 0)


def route_first(replicas, stored_ref, table_ref, failed_ref):
    failed_ref[0] = jnp.int32(0)
    me = lax.axis_index("replica")
    return [stored_ref[0, lax.rem(me + s, replicas)] for s in range(replicas)]


def route_near(stored_ref, table_ref, failed_ref):
    me = lax.axis_index("replica")

    def held(replica):
        return [stored_ref[slot, replica] for slot in range(2)]

    def plan(replica):
        here, after, before = [held(lax.rem(replica + d, 4)) for d in (0, 1, 3)]
        done = jnp.bool_(False)
        slots = [jnp.int32(0), jnp.int32(0)]
        chosen = [after[0], before[0]]
        for i in range(2):
            for k in range(2):
                one, two = after[i], before[k]
                fits = (one != here[0]) & (one != here[1]) & (two != here[0]) & (two != here[1]) & (one != two)
                take = fits & jnp.logical_not(done)
                slots = [jnp.where(take, i, slots[0]), jnp.where(take, k, slots[1])]
                chosen = [jnp.where(take, one, chosen[0]), jnp.where(take, two, chosen[1])]
                done = done | fits
        return slots, chosen, done

    plans = [plan(lax.rem(me + d, 4)) for d in range(4)]
    failed = jnp.int32(0)
    for _, _, done in plans:
        failed = jnp.where(done, failed, 1)
    table_ref[10] = plans[3][0][0]
    table_ref[11] = plans[1][0][1]
    failed_ref[0] = failed
    return held(me) + plans[0][1]


def pack(stored, ids, queries, own, pairs, context, slots, phases, route):
    questions = ids.shape[1]
    head_size = own.shape[1]
    qlength = queries.shape[0] // questions
    heads = queries.shape[1] // head_size
    rows = heads * qlength + 2 * qlength
    arguments = [pltpu.with_memory_space_constraint(x, pltpu.HBM) for x in (stored, ids, queries, own, pairs)]
    split_out, split_scratch = split_shapes(context, head_size, slots)
    out = pl.pallas_call(
        functools.partial(pack_kernel, route=route, heads=heads, qlength=qlength),
        in_specs=[pl.BlockSpec(memory_space=pltpu.HBM)] * 5,
        out_specs=[SMEM, SMEM] + [VMEM] * (phases + 2),
        out_shape=[jax.ShapeDtypeStruct((size,), jnp.int32) for size in (phases * (CAP + 1), 1)]
        + [jax.ShapeDtypeStruct((CAP, rows, head_size), BF16)] * phases
        + split_out,
        scratch_shapes=[
            pltpu.SMEM(stored.shape, jnp.int32),
            pltpu.SMEM(ids.shape, jnp.int32),
            pltpu.VMEM(queries.shape, BF16),
            pltpu.VMEM(own.shape, BF16),
            pltpu.SemaphoreType.DMA((4,)),
            *split_scratch,
        ],
        compiler_params=pltpu.CompilerParams(vmem_limit_bytes=16 << 20),
        cost_estimate=pl.CostEstimate(flops=0, bytes_accessed=4 << 20, transcendentals=0),
        name="pack",
    )(*arguments)
    return out[0], out[1], out[2:-2], out[-2:]


def split_copies(x_ref, pairs_ref, sems, slot):
    parts, block, _ = pairs_ref.shape
    return [
        pltpu.make_async_copy(x_ref.at[pl.ds((slot * parts + i) * block, block), :], pairs_ref.at[i], sems.at[i])
        for i in range(parts)
    ]


def split_arrived(copies, k_ref, vt_ref, pairs_ref, wide_ref, slot):
    half, head_size = pairs_ref.shape[1] // 2, pairs_ref.shape[2]
    depth, context = vt_ref.shape[1:]
    vt_ref[slot, head_size:, :] = jnp.ones((depth - head_size, context), BF16)
    for i, copy in enumerate(copies):
        copy.wait()
        wide = wide_ref.at[i % 2]
        wide[...] = pairs_ref[i].astype(F32)
        k_ref[slot, i * half : (i + 1) * half, :] = wide[pl.ds(0, half, stride=2), :].astype(BF16)
        values = wide[pl.ds(1, half, stride=2), :]
        vt_ref[slot, :head_size, i * half : (i + 1) * half] = values.T.astype(BF16)


def split_shapes(context, head_size, slots):
    parts = 8
    block = 2 * context // parts
    out_shape = [
        jax.ShapeDtypeStruct((slots, context, head_size), BF16),
        jax.ShapeDtypeStruct((slots, head_size + 16, context), BF16),
    ]
    scratch_shapes = [
        pltpu.VMEM((parts, block, head_size), BF16),
        pltpu.VMEM((2, block, head_size), F32),
        pltpu.SemaphoreType.DMA((parts,)),
    ]
    return out_shape, scratch_shapes


def split_kernel(x_ref, keys_ref, values_ref, after_ref, k_ref, vt_ref, pairs_ref, wide_ref, sems, *, slot):
    copies = split_copies(x_ref, pairs_ref, sems, slot)
    for copy in copies:
        copy.start()
    split_arrived(copies, k_ref, vt_ref, pairs_ref, wide_ref, slot)


def split(pairs, keys, values_t, slot, after):
    slots, context, head_size = keys.shape
    out_shape, scratch_shapes = split_shapes(context, head_size, slots)
    hbm = pl.BlockSpec(memory_space=pltpu.HBM)
    return pl.pallas_call(
        functools.partial(split_kernel, slot=slot),
        in_specs=[hbm, VMEM, VMEM, pl.BlockSpec(memory_space=pl.ANY)],
        out_specs=[VMEM, VMEM],
        out_shape=out_shape,
        scratch_shapes=scratch_shapes,
        input_output_aliases={1: 0, 2: 1},
        compiler_params=pltpu.CompilerParams(vmem_limit_bytes=16 << 20),
        cost_estimate=pl.CostEstimate(flops=0, bytes_accessed=8 * context * head_size, transcendentals=0),
        name="split",
    )(pltpu.with_memory_space_constraint(pairs, pltpu.HBM), keys, values_t, after)


def attend_kernel(*refs, entry, heads, qlength, chunk):
    if isinstance(entry, int):
        x_ref, keys_ref, values_ref, o_ref = refs
        slot = entry
    else:
        table_ref, x_ref, keys_ref, values_ref, o_ref = refs
        slot = table_ref[entry[0]]
    k_ref, vt_ref = keys_ref.at[slot], values_ref.at[slot]
    context, head_size = k_ref.shape
    scale = LOG2E / math.sqrt(head_size)
    rows = heads * qlength

    def start(i):
        qt = x_ref[i, :rows, :].T
        own = x_ref[i, rows:, :]
        near = jnp.dot(own, qt, preferred_element_type=F32) * scale
        u2 = lax.broadcasted_iota(jnp.int32, near.shape, 0)
        t = lax.broadcasted_iota(jnp.int32, near.shape, 1) % qlength
        near = jnp.where((u2 % 2 == 0) & (u2 <= 2 * t), near, -jnp.inf)
        own_vt = jnp.concatenate([own.astype(F32).T.astype(BF16), jnp.ones((16, own.shape[0]), BF16)], axis=0)

        def mix_near(top):
            weights = pltpu.roll(jnp.exp2(near - top), 1, 0).astype(BF16)
            return jnp.dot(own_vt, weights, preferred_element_type=F32)

        return qt, jnp.max(near, axis=0, keepdims=True), mix_near

    def store(i, mixed):
        result = (mixed[:head_size] / mixed[head_size : head_size + 1]).T.astype(BF16)
        target = pl.ds(i * qlength if isinstance(i, int) else pl.multiple_of(i * qlength, qlength), qlength)
        for h in range(heads):
            o_ref[target, h * head_size : (h + 1) * head_size] = result[h * qlength : (h + 1) * qlength, :]

    def shifted(i):
        qt, top, mix_near = start(i)
        scores = jnp.dot(k_ref[...], qt, preferred_element_type=F32) * scale
        weights = jnp.exp2(scores - top).astype(BF16)
        mixed = jnp.dot(vt_ref[...], weights, preferred_element_type=F32) + mix_near(top)
        store(i, mixed)
        return jnp.where(mixed[head_size : head_size + 1] < TOTAL_MAX, 0.0, 1.0)

    def by_maximum(i, carry):
        qt, top, mix_near = start(i)

        def part(j):
            keys = k_ref[pl.ds(pl.multiple_of(j * chunk, chunk), chunk), :]
            return jnp.dot(keys, qt, preferred_element_type=F32) * scale

        def raise_top(j, top):
            return jnp.maximum(top, jnp.max(part(j), axis=0, keepdims=True))

        top = lax.fori_loop(0, context // chunk, raise_top, top)

        def add(j, mixed):
            weights = jnp.exp2(part(j) - top).astype(BF16)
            values = vt_ref[:, pl.ds(pl.multiple_of(j * chunk, chunk), chunk)]
            return mixed + jnp.dot(values, weights, preferred_element_type=F32)

        store(i, lax.fori_loop(0, context // chunk, add, mix_near(top)))
        return carry

    number = x_ref.shape[0]
    if number == CAP:
        large = functools.reduce(jnp.maximum, [shifted(i) for i in range(number)])
    else:
        large = lax.fori_loop(0, number, lambda i, large: jnp.maximum(large, shifted(i)), jnp.zeros((1, rows), F32))

    @pl.when(jnp.max(large) > 0.5)
    def _():
        lax.fori_loop(0, number, by_maximum, 0)


def attend(table, entry, x, keys, values_t, heads, qlength):
    number, _, head_size = x.shape
    context = keys.shape[1]
    tables = [] if isinstance(entry, int) else [table]
    return pl.pallas_call(
        functools.partial(attend_kernel, entry=entry, heads=heads, qlength=qlength, chunk=512),
        in_specs=[SMEM] * len(tables) + [VMEM, VMEM, VMEM],
        out_specs=VMEM,
        out_shape=jax.ShapeDtypeStruct((number * qlength, heads * head_size), BF16),
        compiler_params=pltpu.CompilerParams(vmem_limit_bytes=20 << 20),
        cost_estimate=pl.CostEstimate(
            flops=8 * number * qlength * heads * context * head_size,
            bytes_accessed=4 << 20,
            transcendentals=number * qlength * heads * context,
        ),
        name="attend",
    )(*tables, x, keys, values_t)


def project_kernel(a_ref, w_ref, *out_refs, flips, tile):
    columns = out_refs[0].shape[1]
    me = lax.axis_index("tensor")

    def one(i, carry):
        out = pl.ds(pl.multiple_of(i * tile, tile), tile)
        for ref, flip in zip(out_refs, flips):
            source = pl.ds(pl.multiple_of((me ^ flip) * columns + i * tile, tile), tile)
            product = jnp.dot(a_ref[...], w_ref[:, source], preferred_element_type=F32)
            ref[:, out] = product.astype(ref.dtype)
        return carry

    lax.fori_loop(0, columns // tile, one, 0)


def project(rows, weight, shares, tile, flips, types):
    number, depth = rows.shape
    columns = weight.shape[1] // shares
    return pl.pallas_call(
        functools.partial(project_kernel, flips=flips, tile=tile),
        in_specs=[VMEM, VMEM],
        out_specs=[VMEM] * len(flips),
        out_shape=[jax.ShapeDtypeStruct((number, columns), kind) for kind in types],
        compiler_params=pltpu.CompilerParams(vmem_limit_bytes=12 << 20),
        cost_estimate=pl.CostEstimate(
            flops=2 * len(flips) * number * depth * columns,
            bytes_accessed=2 * len(flips) * depth * columns,
            transcendentals=0,
        ),
        name="project",
    )(rows, weight)


def finish_kernel(table_ref, counts_ref, kept_ref, core_ref, far_ref, *refs, first, qlength, tile):
    o_ref, block_ref, sems = refs[-3:]
    number, _, columns = block_ref.shape
    places = [jnp.maximum(table_ref[first + i], 0) for i in range(number)]
    counts = [counts_ref[0, place] for place in places]
    t = lax.broadcasted_iota(jnp.int32, (qlength, tile), 0)

    def one(j, carry):
        out = pl.ds(pl.multiple_of(j * tile, tile), tile)
        total = kept_ref[:, out] + core_ref[:, out].astype(F32) + far_ref[:, out].astype(F32)
        for i in range(number):
            block = total[i * qlength : (i + 1) * qlength, :]
            block_ref[i, :, out] = jnp.where(t < counts[i], block, 0.0).astype(BF16)
        return carry

    lax.fori_loop(0, columns // tile, one, 0)
    copies = []
    for i, place in enumerate(places):
        target = o_ref.at[pl.ds(pl.multiple_of(place * qlength, qlength), qlength), :]
        copies.append(pltpu.make_async_copy(block_ref.at[i], target, sems.at[i]))
        copies[-1].start()
    for copy in copies:
        copy.wait()


def finish(table, counts, kept, from_core, from_far, first, previous, rows, qlength, tile):
    number, columns = kept.shape[0] // qlength, kept.shape[1]
    extra = [] if previous is None else [pltpu.with_memory_space_constraint(previous, pltpu.HBM)]
    hbm = pl.BlockSpec(memory_space=pltpu.HBM)
    return pl.pallas_call(
        functools.partial(finish_kernel, first=first, qlength=qlength, tile=tile),
        in_specs=[SMEM, SMEM, VMEM, VMEM, VMEM] + [hbm] * len(extra),
        out_specs=hbm,
        out_shape=pltpu.HBM((rows, columns), BF16),
        scratch_shapes=[pltpu.VMEM((number, qlength, columns), BF16), pltpu.SemaphoreType.DMA((number,))],
        input_output_aliases={5: 0} if extra else {},
        compiler_params=pltpu.CompilerParams(vmem_limit_bytes=12 << 20),
        cost_estimate=pl.CostEstimate(flops=0, bytes_accessed=10 * kept.shape[0] * columns, transcendentals=0),
        name="finish",
    )(table, counts, kept, from_core, from_far, *extra)


def by_shift(shift, replicas):
    return [(i, (i + shift) % replicas) for i in range(replicas)]


def small_slice(groups, replicas, shares):
    return groups <= 2 and replicas == 4 and shares == 4


def project_out(table, counts, results, weight, shares, first, out, rows, qlength):
    other_core = [(i, i ^ 1) for i in range(shares)]
    other_chip = [(i, i ^ 2) for i in range(shares)]
    tile = 512
    far_give, far_keep = project(results, weight, shares, tile, (3, 2), (BF16, F32))
    far_core = lax.ppermute(far_give, "tensor", other_core)
    (near_give,) = project(results, weight, shares, tile, (1,), (BF16,))
    near_core = lax.ppermute(near_give, "tensor", other_core)
    chip_sum = (far_keep + far_core.astype(F32)).astype(BF16)
    far = lax.ppermute(chip_sum, "tensor", other_chip)
    (near_keep,) = project(results, weight, shares, tile, (0,), (F32,))
    return finish(table, counts, near_keep, near_core, far, first, out, rows, qlength, tile)


def answer_by_first_slots(queries, own, pairs, context, stored, ids, heads, qlength):
    replicas = stored.shape[1]
    route = functools.partial(route_first, replicas)
    table, _, packed, (keys, values_t) = pack(stored, ids, queries, own, pairs, context, 1, replicas, route)
    arrived = [packed[0]] + [lax.ppermute(packed[s], "replica", by_shift(s, replicas)) for s in range(1, replicas)]
    result = attend(table, 0, jnp.concatenate(arrived), keys, values_t, heads, qlength)
    parts = result.reshape(replicas, CAP * qlength, -1)
    returned = [parts[0]] + [lax.ppermute(parts[s], "replica", by_shift(-s, replicas)) for s in range(1, replicas)]
    return table, jnp.concatenate(returned)


def on_device(queries, new_kv, cache_kv, stored, haystack_ids, token_counts, out_weight):
    groups = lax.axis_size("groups")
    replicas = lax.axis_size("replica")
    shares = lax.axis_size("tensor")
    slots, context = cache_kv.shape[:2]
    head_size = cache_kv.shape[-1]
    questions = haystack_ids.shape[0]
    rows = queries.shape[0]
    qlength = rows // questions
    heads = queries.shape[1] // head_size
    own = new_kv.reshape(2 * rows, head_size)
    pairs = cache_kv.reshape(-1, head_size)
    ids = haystack_ids.T
    stored = stored.T

    if small_slice(groups, replicas, shares) and replicas * CAP == questions and slots == 2:
        table, failed, packed, (keys, values_t) = pack(
            stored, ids, queries, own, pairs, context, slots, 4, route_near
        )
        arrived, returned = dict(enumerate(packed)), {}
        shifts = {2: 1, 3: -1}
        for s, shift in shifts.items():
            arrived[s] = lax.ppermute(packed[s], "replica", by_shift(shift, replicas))
        for s in range(4):
            if s == 1:
                keys, values_t = split(pairs, keys, values_t, 1, returned[0])
            returned[s] = attend(table, s if s < 2 else (8 + s,), arrived[s], keys, values_t, heads, qlength)
            if s in shifts:
                returned[s] = lax.ppermute(returned[s], "replica", by_shift(-shifts[s], replicas))
        out = None
        for s in range(4):
            out = project_out(table, token_counts, returned[s], out_weight, shares, s * CAP, out, rows, qlength)

        def again():
            table, results = answer_by_first_slots(queries, own, pairs, context, stored, ids, heads, qlength)
            return project_out(table, token_counts, results, out_weight, shares, 0, None, rows, qlength)

        return lax.cond(failed[0] > 0, again, lambda: out)

    table, results = answer_by_first_slots(queries, own, pairs, context, stored, ids, heads, qlength)
    blocks = results.reshape(replicas * CAP, qlength, -1)
    match = table[None, : replicas * CAP] == jnp.arange(questions, dtype=jnp.int32)[:, None]
    position = jnp.argmax(match.astype(jnp.int32), axis=1)
    used = jnp.arange(qlength, dtype=jnp.int32)[None, :] < token_counts[0][:, None]
    attended = jnp.where(used[..., None], blocks[position], jnp.zeros((), BF16)).reshape(rows, -1)
    summed = lax.psum_scatter(
        lax.dot_general(out_weight, attended, (((0,), (1,)), ((), ())), preferred_element_type=F32),
        "tensor",
        scatter_dimension=0,
        tiled=True,
    )
    return summed.T.astype(BF16)


def solution(mesh):
    in_specs = (
        P(("groups", "replica"), "tensor"),
        P(("groups", "replica"), None, "tensor"),
        P(("groups", "replica"), None, None, "tensor"),
        P("groups", None),
        P(("groups", "replica"), None),
        P(("groups", "replica"), None),
        P("tensor", None),
    )
    out_specs = P(("groups", "replica"), "tensor")
    return jax.shard_map(
        on_device, mesh=mesh, in_specs=in_specs, out_specs=out_specs, check_vma=False
    )
```

```python
import functools
import math

import jax
import jax.numpy as jnp
from jax import lax
from jax.experimental import pallas as pl
from jax.experimental.pallas import tpu as pltpu
from jax.sharding import PartitionSpec as P


CAP = 2
BF16 = jnp.bfloat16
F32 = jnp.float32
LOG2E = 1.4426950408889634
TOTAL_MAX = 1e30
VMEM = pl.BlockSpec(memory_space=pltpu.VMEM)
SMEM = pl.BlockSpec(memory_space=pltpu.SMEM)


def pack_kernel(
    stored_hbm, ids_hbm, counts_hbm, q_hbm, own_hbm, kv_hbm, table_ref, failed_ref, slots_ref, *refs, route, heads, qlength
):
    number = len(refs) - 11
    out_refs, (k_ref, vt_ref) = refs[:number], refs[number : number + 2]
    stored_ref, ids_ref, counts_ref, q_ref, own_ref, sems, pairs_ref, wide_ref, kv_sems = refs[number + 2 :]
    head_size = own_ref.shape[1]
    questions = ids_ref.shape[1]
    pairs = ((stored_hbm, stored_ref), (ids_hbm, ids_ref), (counts_hbm, counts_ref), (q_hbm, q_ref), (own_hbm, own_ref))
    copies = [pltpu.make_async_copy(source, target, sems.at[i]) for i, (source, target) in enumerate(pairs)]
    kv_copies = split_copies(kv_hbm, pairs_ref, kv_sems, 0)
    for copy in copies + kv_copies:
        copy.start()
    for copy in copies[:3]:
        copy.wait()
    places = []
    for s, haystack in enumerate(route(stored_ref, slots_ref, failed_ref)):
        count = jnp.int32(0)
        found = [jnp.int32(-1)] * CAP
        for i in range(questions):
            hit = ids_ref[0, i] == haystack
            for j in range(CAP):
                found[j] = jnp.where(hit & (count == j), jnp.int32(i), found[j])
            count = count + hit.astype(jnp.int32)
        for j in range(CAP):
            table_ref[s * CAP + j] = found[j]
        places.append([jnp.maximum(place, 0) for place in found])
        for j, place in enumerate(places[s]):
            table_ref[(number + s) * CAP + j] = counts_ref[0, place]
    for copy in copies[3:]:
        copy.wait()
    for s, out_ref in enumerate(out_refs):
        for j, place in enumerate(places[s]):
            rows = q_ref[pl.ds(pl.multiple_of(place * qlength, qlength), qlength), :]
            for h in range(heads):
                out_ref[j, h * qlength : (h + 1) * qlength, :] = rows[:, h * head_size : (h + 1) * head_size]
            own = own_ref[pl.ds(pl.multiple_of(place * 2 * qlength, 2 * qlength), 2 * qlength), :]
            out_ref[j, heads * qlength :, :] = own
    split_arrived(kv_copies, k_ref, vt_ref, pairs_ref, wide_ref, 0)


def route_first(replicas, stored_ref, slots_ref, failed_ref):
    failed_ref[0] = jnp.int32(0)
    slots_ref[...] = jnp.zeros_like(slots_ref)
    me = lax.axis_index("replica")
    return [stored_ref[0, lax.rem(me + s, replicas)] for s in range(replicas)]


def route_near(stored_ref, slots_ref, failed_ref):
    me = lax.axis_index("replica")

    def held(replica):
        return [stored_ref[slot, replica] for slot in range(2)]

    def plan(replica):
        here, after, before = [held(lax.rem(replica + d, 4)) for d in (0, 1, 3)]
        done = jnp.bool_(False)
        slots = [jnp.int32(0), jnp.int32(0)]
        chosen = [after[0], before[0]]
        for i in range(2):
            for k in range(2):
                one, two = after[i], before[k]
                fits = (one != here[0]) & (one != here[1]) & (two != here[0]) & (two != here[1]) & (one != two)
                take = fits & jnp.logical_not(done)
                slots = [jnp.where(take, i, slots[0]), jnp.where(take, k, slots[1])]
                chosen = [jnp.where(take, one, chosen[0]), jnp.where(take, two, chosen[1])]
                done = done | fits
        return slots, chosen, done

    plans = [plan(lax.rem(me + d, 4)) for d in range(4)]
    failed = jnp.int32(0)
    for _, _, done in plans:
        failed = jnp.where(done, failed, 1)
    for i, slot in enumerate((plans[3][0][0], plans[1][0][1])):
        slots_ref[i] = jnp.full(slots_ref.shape[1:], slot, jnp.int32).astype(F32)
    failed_ref[0] = failed
    return held(me) + plans[0][1]


def pack(stored, ids, counts, queries, own, pairs, context, slots, phases, route):
    questions = ids.shape[1]
    head_size = own.shape[1]
    qlength = queries.shape[0] // questions
    heads = queries.shape[1] // head_size
    rows = heads * qlength + 2 * qlength
    arguments = [pltpu.with_memory_space_constraint(x, pltpu.HBM) for x in (stored, ids, counts, queries, own, pairs)]
    split_out, split_scratch = split_shapes(context, head_size, slots)
    out = pl.pallas_call(
        functools.partial(pack_kernel, route=route, heads=heads, qlength=qlength),
        in_specs=[pl.BlockSpec(memory_space=pltpu.HBM)] * 6,
        out_specs=[SMEM, SMEM] + [VMEM] * (phases + 3),
        out_shape=[jax.ShapeDtypeStruct((size,), jnp.int32) for size in (2 * phases * CAP, 1)]
        + [jax.ShapeDtypeStruct((2, 8, 128), F32)]
        + [jax.ShapeDtypeStruct((CAP, rows, head_size), BF16)] * phases
        + split_out,
        scratch_shapes=[
            pltpu.SMEM(stored.shape, jnp.int32),
            pltpu.SMEM(ids.shape, jnp.int32),
            pltpu.SMEM(counts.shape, jnp.int32),
            pltpu.VMEM(queries.shape, BF16),
            pltpu.VMEM(own.shape, BF16),
            pltpu.SemaphoreType.DMA((5,)),
            *split_scratch,
        ],
        compiler_params=pltpu.CompilerParams(vmem_limit_bytes=16 << 20),
        cost_estimate=pl.CostEstimate(flops=0, bytes_accessed=4 << 20, transcendentals=0),
        name="pack",
    )(*arguments)
    return *out[:3], out[3:-2], out[-2:]


def split_copies(x_ref, pairs_ref, sems, slot):
    parts, block, _ = pairs_ref.shape
    return [
        pltpu.make_async_copy(x_ref.at[pl.ds((slot * parts + i) * block, block), :], pairs_ref.at[i], sems.at[i])
        for i in range(parts)
    ]


def split_arrived(copies, k_ref, vt_ref, pairs_ref, wide_ref, slot):
    half, head_size = pairs_ref.shape[1] // 2, pairs_ref.shape[2]
    depth, context = vt_ref.shape[1:]
    vt_ref[slot, head_size:, :] = jnp.ones((depth - head_size, context), BF16)
    for i, copy in enumerate(copies):
        copy.wait()
        wide = wide_ref.at[i % 2]
        wide[...] = pairs_ref[i].astype(F32)
        k_ref[slot, i * half : (i + 1) * half, :] = wide[pl.ds(0, half, stride=2), :].astype(BF16)
        values = wide[pl.ds(1, half, stride=2), :]
        vt_ref[slot, :head_size, i * half : (i + 1) * half] = values.T.astype(BF16)


def split_shapes(context, head_size, slots):
    parts = 8
    block = 2 * context // parts
    out_shape = [
        jax.ShapeDtypeStruct((slots, context, head_size), BF16),
        jax.ShapeDtypeStruct((slots, head_size + 16, context), BF16),
    ]
    scratch_shapes = [
        pltpu.VMEM((parts, block, head_size), BF16),
        pltpu.VMEM((2, block, head_size), F32),
        pltpu.SemaphoreType.DMA((parts,)),
    ]
    return out_shape, scratch_shapes


def split_kernel(x_ref, keys_ref, values_ref, after_ref, k_ref, vt_ref, pairs_ref, wide_ref, sems, *, slot):
    copies = split_copies(x_ref, pairs_ref, sems, slot)
    for copy in copies:
        copy.start()
    split_arrived(copies, k_ref, vt_ref, pairs_ref, wide_ref, slot)


def split(pairs, keys, values_t, slot, after):
    slots, context, head_size = keys.shape
    out_shape, scratch_shapes = split_shapes(context, head_size, slots)
    hbm = pl.BlockSpec(memory_space=pltpu.HBM)
    return pl.pallas_call(
        functools.partial(split_kernel, slot=slot),
        in_specs=[hbm, VMEM, VMEM, pl.BlockSpec(memory_space=pl.ANY)],
        out_specs=[VMEM, VMEM],
        out_shape=out_shape,
        scratch_shapes=scratch_shapes,
        input_output_aliases={1: 0, 2: 1},
        compiler_params=pltpu.CompilerParams(vmem_limit_bytes=16 << 20),
        cost_estimate=pl.CostEstimate(flops=0, bytes_accessed=8 * context * head_size, transcendentals=0),
        name="split",
    )(pltpu.with_memory_space_constraint(pairs, pltpu.HBM), keys, values_t, after)


def attend_kernel(*refs, entry, heads, qlength, chunk):
    if isinstance(entry, int):
        x_ref, keys_ref, values_ref, o_ref = refs
        slot = entry
    else:
        slots_ref, x_ref, keys_ref, values_ref, o_ref = refs
        slot = jnp.max(slots_ref[entry[0]]).astype(jnp.int32)
    k_ref, vt_ref = keys_ref.at[slot], values_ref.at[slot]
    context, head_size = k_ref.shape
    scale = LOG2E / math.sqrt(head_size)
    rows = heads * qlength

    def start(i):
        qt = x_ref[i, :rows, :].T
        own = x_ref[i, rows:, :]
        near = jnp.dot(own, qt, preferred_element_type=F32) * scale
        u2 = lax.broadcasted_iota(jnp.int32, near.shape, 0)
        t = lax.broadcasted_iota(jnp.int32, near.shape, 1) % qlength
        near = jnp.where((u2 % 2 == 0) & (u2 <= 2 * t), near, -jnp.inf)
        own_vt = jnp.concatenate([own.astype(F32).T.astype(BF16), jnp.ones((16, own.shape[0]), BF16)], axis=0)

        def mix_near(top):
            weights = pltpu.roll(jnp.exp2(near - top), 1, 0).astype(BF16)
            return jnp.dot(own_vt, weights, preferred_element_type=F32)

        return qt, jnp.max(near, axis=0, keepdims=True), mix_near

    def store(i, mixed):
        result = (mixed[:head_size] / mixed[head_size : head_size + 1]).T.astype(BF16)
        target = pl.ds(i * qlength if isinstance(i, int) else pl.multiple_of(i * qlength, qlength), qlength)
        for h in range(heads):
            o_ref[target, h * head_size : (h + 1) * head_size] = result[h * qlength : (h + 1) * qlength, :]

    def shifted(i):
        qt, top, mix_near = start(i)
        scores = jnp.dot(k_ref[...], qt, preferred_element_type=F32) * scale
        weights = jnp.exp2(scores - top).astype(BF16)
        mixed = jnp.dot(vt_ref[...], weights, preferred_element_type=F32) + mix_near(top)
        store(i, mixed)
        return jnp.where(mixed[head_size : head_size + 1] < TOTAL_MAX, 0.0, 1.0)

    def by_maximum(i, carry):
        qt, top, mix_near = start(i)

        def part(j):
            keys = k_ref[pl.ds(pl.multiple_of(j * chunk, chunk), chunk), :]
            return jnp.dot(keys, qt, preferred_element_type=F32) * scale

        def raise_top(j, top):
            return jnp.maximum(top, jnp.max(part(j), axis=0, keepdims=True))

        top = lax.fori_loop(0, context // chunk, raise_top, top)

        def add(j, mixed):
            weights = jnp.exp2(part(j) - top).astype(BF16)
            values = vt_ref[:, pl.ds(pl.multiple_of(j * chunk, chunk), chunk)]
            return mixed + jnp.dot(values, weights, preferred_element_type=F32)

        store(i, lax.fori_loop(0, context // chunk, add, mix_near(top)))
        return carry

    number = x_ref.shape[0]
    if number == CAP:
        large = functools.reduce(jnp.maximum, [shifted(i) for i in range(number)])
    else:
        large = lax.fori_loop(0, number, lambda i, large: jnp.maximum(large, shifted(i)), jnp.zeros((1, rows), F32))

    @pl.when(jnp.max(large) > 0.5)
    def _():
        lax.fori_loop(0, number, by_maximum, 0)


def attend(slots, entry, x, keys, values_t, heads, qlength):
    number, _, head_size = x.shape
    context = keys.shape[1]
    tables = [] if isinstance(entry, int) else [slots]
    return pl.pallas_call(
        functools.partial(attend_kernel, entry=entry, heads=heads, qlength=qlength, chunk=512),
        in_specs=[VMEM] * (len(tables) + 3),
        out_specs=VMEM,
        out_shape=jax.ShapeDtypeStruct((number * qlength, heads * head_size), BF16),
        compiler_params=pltpu.CompilerParams(vmem_limit_bytes=20 << 20),
        cost_estimate=pl.CostEstimate(
            flops=8 * number * qlength * heads * context * head_size,
            bytes_accessed=4 << 20,
            transcendentals=number * qlength * heads * context,
        ),
        name="attend",
    )(*tables, x, keys, values_t)


def project_kernel(a_ref, w_ref, *out_refs, flips, tile):
    columns = out_refs[0].shape[1]
    me = lax.axis_index("tensor")

    def one(i, carry):
        out = pl.ds(pl.multiple_of(i * tile, tile), tile)
        for ref, flip in zip(out_refs, flips):
            source = pl.ds(pl.multiple_of((me ^ flip) * columns + i * tile, tile), tile)
            product = jnp.dot(a_ref[...], w_ref[:, source], preferred_element_type=F32)
            ref[:, out] = product.astype(ref.dtype)
        return carry

    lax.fori_loop(0, columns // tile, one, 0)


def project(rows, weight, shares, tile, flips, types):
    number, depth = rows.shape
    columns = weight.shape[1] // shares
    return pl.pallas_call(
        functools.partial(project_kernel, flips=flips, tile=tile),
        in_specs=[VMEM, VMEM],
        out_specs=[VMEM] * len(flips),
        out_shape=[jax.ShapeDtypeStruct((number, columns), kind) for kind in types],
        compiler_params=pltpu.CompilerParams(vmem_limit_bytes=12 << 20),
        cost_estimate=pl.CostEstimate(
            flops=2 * len(flips) * number * depth * columns,
            bytes_accessed=2 * len(flips) * depth * columns,
            transcendentals=0,
        ),
        name="project",
    )(rows, weight)


def finish_kernel(table_ref, kept_ref, core_ref, far_ref, *refs, first, qlength, tile):
    o_ref, block_ref, sems = refs[-3:]
    number, _, columns = block_ref.shape
    places = [jnp.maximum(table_ref[first + i], 0) for i in range(number)]
    counts = [table_ref[table_ref.shape[0] // 2 + first + i] for i in range(number)]
    t = lax.broadcasted_iota(jnp.int32, (qlength, tile), 0)

    def one(j, carry):
        out = pl.ds(pl.multiple_of(j * tile, tile), tile)
        total = kept_ref[:, out] + core_ref[:, out].astype(F32) + far_ref[:, out].astype(F32)
        for i in range(number):
            block = total[i * qlength : (i + 1) * qlength, :]
            block_ref[i, :, out] = jnp.where(t < counts[i], block, 0.0).astype(BF16)
        return carry

    lax.fori_loop(0, columns // tile, one, 0)
    copies = []
    for i, place in enumerate(places):
        target = o_ref.at[pl.ds(pl.multiple_of(place * qlength, qlength), qlength), :]
        copies.append(pltpu.make_async_copy(block_ref.at[i], target, sems.at[i]))
        copies[-1].start()
    for copy in copies:
        copy.wait()


def finish(table, kept, from_core, from_far, first, previous, rows, qlength, tile):
    number, columns = kept.shape[0] // qlength, kept.shape[1]
    extra = [] if previous is None else [pltpu.with_memory_space_constraint(previous, pltpu.HBM)]
    hbm = pl.BlockSpec(memory_space=pltpu.HBM)
    return pl.pallas_call(
        functools.partial(finish_kernel, first=first, qlength=qlength, tile=tile),
        in_specs=[SMEM, VMEM, VMEM, VMEM] + [hbm] * len(extra),
        out_specs=hbm,
        out_shape=pltpu.HBM((rows, columns), BF16),
        scratch_shapes=[pltpu.VMEM((number, qlength, columns), BF16), pltpu.SemaphoreType.DMA((number,))],
        input_output_aliases={4: 0} if extra else {},
        compiler_params=pltpu.CompilerParams(vmem_limit_bytes=12 << 20),
        cost_estimate=pl.CostEstimate(flops=0, bytes_accessed=10 * kept.shape[0] * columns, transcendentals=0),
        name="finish",
    )(table, kept, from_core, from_far, *extra)


def by_shift(shift, replicas):
    return [(i, (i + shift) % replicas) for i in range(replicas)]


def small_slice(groups, replicas, shares):
    return groups <= 2 and replicas == 4 and shares == 4


def project_out(table, results, weight, shares, first, out, rows, qlength):
    other_core = [(i, i ^ 1) for i in range(shares)]
    other_chip = [(i, i ^ 2) for i in range(shares)]
    tile = 512
    far_give, far_keep = project(results, weight, shares, tile, (3, 2), (BF16, F32))
    far_core = lax.ppermute(far_give, "tensor", other_core)
    (near_give,) = project(results, weight, shares, tile, (1,), (BF16,))
    near_core = lax.ppermute(near_give, "tensor", other_core)
    chip_sum = (far_keep + far_core.astype(F32)).astype(BF16)
    far = lax.ppermute(chip_sum, "tensor", other_chip)
    (near_keep,) = project(results, weight, shares, tile, (0,), (F32,))
    return finish(table, near_keep, near_core, far, first, out, rows, qlength, tile)


def answer_by_first_slots(queries, own, pairs, context, stored, ids, counts, heads, qlength):
    replicas = stored.shape[1]
    route = functools.partial(route_first, replicas)
    table, _, _, packed, (keys, values_t) = pack(
        stored, ids, counts, queries, own, pairs, context, 1, replicas, route
    )
    arrived = [packed[0]] + [lax.ppermute(packed[s], "replica", by_shift(s, replicas)) for s in range(1, replicas)]
    result = attend(None, 0, jnp.concatenate(arrived), keys, values_t, heads, qlength)
    parts = result.reshape(replicas, CAP * qlength, -1)
    returned = [parts[0]] + [lax.ppermute(parts[s], "replica", by_shift(-s, replicas)) for s in range(1, replicas)]
    return table, jnp.concatenate(returned)


def on_device(queries, new_kv, cache_kv, stored, haystack_ids, token_counts, out_weight):
    groups = lax.axis_size("groups")
    replicas = lax.axis_size("replica")
    shares = lax.axis_size("tensor")
    slots, context = cache_kv.shape[:2]
    head_size = cache_kv.shape[-1]
    questions = haystack_ids.shape[0]
    rows = queries.shape[0]
    qlength = rows // questions
    heads = queries.shape[1] // head_size
    own = new_kv.reshape(2 * rows, head_size)
    pairs = cache_kv.reshape(-1, head_size)
    ids = haystack_ids.T
    stored = stored.T

    if small_slice(groups, replicas, shares) and replicas * CAP == questions and slots == 2:
        table, failed, chosen, packed, (keys, values_t) = pack(
            stored, ids, token_counts, queries, own, pairs, context, slots, 4, route_near
        )
        arrived, returned = dict(enumerate(packed)), {}
        shifts = {2: 1, 3: -1}
        for s, shift in shifts.items():
            arrived[s] = lax.ppermute(packed[s], "replica", by_shift(shift, replicas))
        for s in range(4):
            if s == 1:
                keys, values_t = split(pairs, keys, values_t, 1, returned[0])
            returned[s] = attend(chosen, s if s < 2 else (s - 2,), arrived[s], keys, values_t, heads, qlength)
            if s in shifts:
                returned[s] = lax.ppermute(returned[s], "replica", by_shift(-shifts[s], replicas))
        out = None
        for s in range(4):
            out = project_out(table, returned[s], out_weight, shares, s * CAP, out, rows, qlength)

        def again():
            table, results = answer_by_first_slots(queries, own, pairs, context, stored, ids, token_counts, heads, qlength)
            return project_out(table, results, out_weight, shares, 0, None, rows, qlength)

        return lax.cond(failed[0] > 0, again, lambda: out)

    table, results = answer_by_first_slots(queries, own, pairs, context, stored, ids, token_counts, heads, qlength)
    blocks = results.reshape(replicas * CAP, qlength, -1)
    match = table[None, : replicas * CAP] == jnp.arange(questions, dtype=jnp.int32)[:, None]
    position = jnp.argmax(match.astype(jnp.int32), axis=1)
    used = jnp.arange(qlength, dtype=jnp.int32)[None, :] < token_counts[0][:, None]
    attended = jnp.where(used[..., None], blocks[position], jnp.zeros((), BF16)).reshape(rows, -1)
    summed = lax.psum_scatter(
        lax.dot_general(out_weight, attended, (((0,), (1,)), ((), ())), preferred_element_type=F32),
        "tensor",
        scatter_dimension=0,
        tiled=True,
    )
    return summed.T.astype(BF16)


def solution(mesh):
    in_specs = (
        P(("groups", "replica"), "tensor"),
        P(("groups", "replica"), None, "tensor"),
        P(("groups", "replica"), None, None, "tensor"),
        P("groups", None),
        P(("groups", "replica"), None),
        P(("groups", "replica"), None),
        P("tensor", None),
    )
    out_specs = P(("groups", "replica"), "tensor")
    return jax.shard_map(
        on_device, mesh=mesh, in_specs=in_specs, out_specs=out_specs, check_vma=False
    )
```

```python
import functools
import math

import jax
import jax.numpy as jnp
from jax import lax
from jax.experimental import pallas as pl
from jax.experimental.pallas import tpu as pltpu
from jax.sharding import PartitionSpec as P


CAP = 2
BF16 = jnp.bfloat16
F32 = jnp.float32
LOG2E = 1.4426950408889634
TOTAL_MAX = 1e30
VMEM = pl.BlockSpec(memory_space=pltpu.VMEM)
SMEM = pl.BlockSpec(memory_space=pltpu.SMEM)


def pack_kernel(
    stored_hbm, ids_hbm, counts_hbm, q_hbm, own_hbm, kv_hbm, table_ref, failed_ref, slots_ref, *refs, route, heads, qlength
):
    number = len(refs) - 11
    out_refs, (k_ref, vt_ref) = refs[:number], refs[number : number + 2]
    stored_ref, ids_ref, counts_ref, q_ref, own_ref, sems, pairs_ref, wide_ref, kv_sems = refs[number + 2 :]
    head_size = own_ref.shape[1]
    questions = ids_ref.shape[1]
    pairs = ((stored_hbm, stored_ref), (ids_hbm, ids_ref), (counts_hbm, counts_ref), (q_hbm, q_ref), (own_hbm, own_ref))
    copies = [pltpu.make_async_copy(source, target, sems.at[i]) for i, (source, target) in enumerate(pairs)]
    kv_copies = split_copies(kv_hbm, pairs_ref, kv_sems, 0)
    for copy in copies + kv_copies:
        copy.start()
    for copy in copies[:3]:
        copy.wait()
    places = []
    for s, haystack in enumerate(route(stored_ref, slots_ref, failed_ref)):
        count = jnp.int32(0)
        found = [jnp.int32(-1)] * CAP
        for i in range(questions):
            hit = ids_ref[0, i] == haystack
            for j in range(CAP):
                found[j] = jnp.where(hit & (count == j), jnp.int32(i), found[j])
            count = count + hit.astype(jnp.int32)
        for j in range(CAP):
            table_ref[s * CAP + j] = found[j]
        places.append([jnp.maximum(place, 0) for place in found])
        for j, place in enumerate(places[s]):
            table_ref[(number + s) * CAP + j] = counts_ref[0, place]
    for copy in copies[3:]:
        copy.wait()
    for s, out_ref in enumerate(out_refs):
        for j, place in enumerate(places[s]):
            rows = q_ref[pl.ds(pl.multiple_of(place * qlength, qlength), qlength), :]
            for h in range(heads):
                out_ref[j, h * qlength : (h + 1) * qlength, :] = rows[:, h * head_size : (h + 1) * head_size]
            own = own_ref[pl.ds(pl.multiple_of(place * 2 * qlength, 2 * qlength), 2 * qlength), :]
            out_ref[j, heads * qlength :, :] = own
    split_arrived(kv_copies, k_ref, vt_ref, pairs_ref, wide_ref, 0)


def route_first(replicas, stored_ref, slots_ref, failed_ref):
    failed_ref[0] = jnp.int32(0)
    slots_ref[...] = jnp.zeros_like(slots_ref)
    me = lax.axis_index("replica")
    return [stored_ref[0, lax.rem(me + s, replicas)] for s in range(replicas)]


def route_near(stored_ref, slots_ref, failed_ref):
    me = lax.axis_index("replica")

    def held(replica):
        return [stored_ref[slot, replica] for slot in range(2)]

    def plan(replica):
        here, after, before = [held(lax.rem(replica + d, 4)) for d in (0, 1, 3)]
        done = jnp.bool_(False)
        slots = [jnp.int32(0), jnp.int32(0)]
        chosen = [after[0], before[0]]
        for i in range(2):
            for k in range(2):
                one, two = after[i], before[k]
                fits = (one != here[0]) & (one != here[1]) & (two != here[0]) & (two != here[1]) & (one != two)
                take = fits & jnp.logical_not(done)
                slots = [jnp.where(take, i, slots[0]), jnp.where(take, k, slots[1])]
                chosen = [jnp.where(take, one, chosen[0]), jnp.where(take, two, chosen[1])]
                done = done | fits
        return slots, chosen, done

    plans = [plan(lax.rem(me + d, 4)) for d in range(4)]
    failed = jnp.int32(0)
    for _, _, done in plans:
        failed = jnp.where(done, failed, 1)
    for i, slot in enumerate((plans[3][0][0], plans[1][0][1])):
        slots_ref[i] = jnp.full(slots_ref.shape[1:], slot, jnp.int32).astype(F32)
    failed_ref[0] = failed
    return held(me) + plans[0][1]


def pack(stored, ids, counts, queries, own, pairs, context, slots, phases, route):
    questions = ids.shape[1]
    head_size = own.shape[1]
    qlength = queries.shape[0] // questions
    heads = queries.shape[1] // head_size
    rows = heads * qlength + 2 * qlength
    arguments = [pltpu.with_memory_space_constraint(x, pltpu.HBM) for x in (stored, ids, counts, queries, own, pairs)]
    split_out, split_scratch = split_shapes(context, head_size, slots)
    out = pl.pallas_call(
        functools.partial(pack_kernel, route=route, heads=heads, qlength=qlength),
        in_specs=[pl.BlockSpec(memory_space=pltpu.HBM)] * 6,
        out_specs=[SMEM, SMEM] + [VMEM] * (phases + 3),
        out_shape=[jax.ShapeDtypeStruct((size,), jnp.int32) for size in (2 * phases * CAP, 1)]
        + [jax.ShapeDtypeStruct((2, 8, 128), F32)]
        + [jax.ShapeDtypeStruct((CAP, rows, head_size), BF16)] * phases
        + split_out,
        scratch_shapes=[
            pltpu.SMEM(stored.shape, jnp.int32),
            pltpu.SMEM(ids.shape, jnp.int32),
            pltpu.SMEM(counts.shape, jnp.int32),
            pltpu.VMEM(queries.shape, BF16),
            pltpu.VMEM(own.shape, BF16),
            pltpu.SemaphoreType.DMA((5,)),
            *split_scratch,
        ],
        compiler_params=pltpu.CompilerParams(vmem_limit_bytes=16 << 20),
        cost_estimate=pl.CostEstimate(flops=0, bytes_accessed=4 << 20, transcendentals=0),
        name="pack",
    )(*arguments)
    return *out[:3], out[3:-2], out[-2:]


def split_copies(x_ref, pairs_ref, sems, slot):
    parts, block, _ = pairs_ref.shape
    return [
        pltpu.make_async_copy(x_ref.at[pl.ds((slot * parts + i) * block, block), :], pairs_ref.at[i], sems.at[i])
        for i in range(parts)
    ]


def split_arrived(copies, k_ref, vt_ref, pairs_ref, wide_ref, slot):
    half, head_size = pairs_ref.shape[1] // 2, pairs_ref.shape[2]
    depth, context = vt_ref.shape[1:]
    vt_ref[slot, head_size:, :] = jnp.ones((depth - head_size, context), BF16)
    for i, copy in enumerate(copies):
        copy.wait()
        wide = wide_ref.at[i % 2]
        wide[...] = pairs_ref[i].astype(F32)
        k_ref[slot, i * half : (i + 1) * half, :] = wide[pl.ds(0, half, stride=2), :].astype(BF16)
        values = wide[pl.ds(1, half, stride=2), :]
        vt_ref[slot, :head_size, i * half : (i + 1) * half] = values.T.astype(BF16)


def split_shapes(context, head_size, slots):
    parts = 8
    block = 2 * context // parts
    out_shape = [
        jax.ShapeDtypeStruct((slots, context, head_size), BF16),
        jax.ShapeDtypeStruct((slots, head_size + 16, context), BF16),
    ]
    scratch_shapes = [
        pltpu.VMEM((parts, block, head_size), BF16),
        pltpu.VMEM((2, block, head_size), F32),
        pltpu.SemaphoreType.DMA((parts,)),
    ]
    return out_shape, scratch_shapes


def split_kernel(x_ref, keys_ref, values_ref, after_ref, k_ref, vt_ref, pairs_ref, wide_ref, sems, *, slot):
    copies = split_copies(x_ref, pairs_ref, sems, slot)
    for copy in copies:
        copy.start()
    split_arrived(copies, k_ref, vt_ref, pairs_ref, wide_ref, slot)


def split(pairs, keys, values_t, slot, after):
    slots, context, head_size = keys.shape
    out_shape, scratch_shapes = split_shapes(context, head_size, slots)
    hbm = pl.BlockSpec(memory_space=pltpu.HBM)
    return pl.pallas_call(
        functools.partial(split_kernel, slot=slot),
        in_specs=[hbm, VMEM, VMEM, pl.BlockSpec(memory_space=pl.ANY)],
        out_specs=[VMEM, VMEM],
        out_shape=out_shape,
        scratch_shapes=scratch_shapes,
        input_output_aliases={1: 0, 2: 1},
        compiler_params=pltpu.CompilerParams(vmem_limit_bytes=16 << 20),
        cost_estimate=pl.CostEstimate(flops=0, bytes_accessed=8 * context * head_size, transcendentals=0),
        name="split",
    )(pltpu.with_memory_space_constraint(pairs, pltpu.HBM), keys, values_t, after)


def attend_kernel(*refs, entry, heads, qlength, chunk):
    if isinstance(entry, int):
        x_ref, keys_ref, values_ref, o_ref = refs
        slot = entry
    else:
        slots_ref, x_ref, keys_ref, values_ref, o_ref = refs
        slot = jnp.max(slots_ref[entry[0]]).astype(jnp.int32)
    k_ref, vt_ref = keys_ref.at[slot], values_ref.at[slot]
    context, head_size = k_ref.shape
    scale = LOG2E / math.sqrt(head_size)
    rows = heads * qlength

    def start(i):
        qt = x_ref[i, :rows, :].T
        own = x_ref[i, rows:, :]
        near = jnp.dot(own, qt, preferred_element_type=F32) * scale
        u2 = lax.broadcasted_iota(jnp.int32, near.shape, 0)
        t = lax.broadcasted_iota(jnp.int32, near.shape, 1) % qlength
        near = jnp.where((u2 % 2 == 0) & (u2 <= 2 * t), near, -jnp.inf)
        own_vt = jnp.concatenate([own.astype(F32).T.astype(BF16), jnp.ones((16, own.shape[0]), BF16)], axis=0)

        def mix_near(top):
            weights = pltpu.roll(jnp.exp2(near - top), 1, 0).astype(BF16)
            return jnp.dot(own_vt, weights, preferred_element_type=F32)

        return qt, jnp.max(near, axis=0, keepdims=True), mix_near

    def store(i, mixed):
        result = (mixed[:head_size] / mixed[head_size : head_size + 1]).T.astype(BF16)
        target = pl.ds(i * qlength if isinstance(i, int) else pl.multiple_of(i * qlength, qlength), qlength)
        for h in range(heads):
            o_ref[target, h * head_size : (h + 1) * head_size] = result[h * qlength : (h + 1) * qlength, :]

    def shifted(i):
        qt, top, mix_near = start(i)
        scores = jnp.dot(k_ref[...], qt, preferred_element_type=F32) * scale
        weights = jnp.exp2(scores - top).astype(BF16)
        mixed = jnp.dot(vt_ref[...], weights, preferred_element_type=F32) + mix_near(top)
        store(i, mixed)
        return jnp.where(mixed[head_size : head_size + 1] < TOTAL_MAX, 0.0, 1.0)

    def by_maximum(i, carry):
        qt, top, mix_near = start(i)

        def part(j):
            keys = k_ref[pl.ds(pl.multiple_of(j * chunk, chunk), chunk), :]
            return jnp.dot(keys, qt, preferred_element_type=F32) * scale

        def raise_top(j, top):
            return jnp.maximum(top, jnp.max(part(j), axis=0, keepdims=True))

        top = lax.fori_loop(0, context // chunk, raise_top, top)

        def add(j, mixed):
            weights = jnp.exp2(part(j) - top).astype(BF16)
            values = vt_ref[:, pl.ds(pl.multiple_of(j * chunk, chunk), chunk)]
            return mixed + jnp.dot(values, weights, preferred_element_type=F32)

        store(i, lax.fori_loop(0, context // chunk, add, mix_near(top)))
        return carry

    number = x_ref.shape[0]
    if number == CAP:
        large = functools.reduce(jnp.maximum, [shifted(i) for i in range(number)])
    else:
        large = lax.fori_loop(0, number, lambda i, large: jnp.maximum(large, shifted(i)), jnp.zeros((1, rows), F32))

    @pl.when(jnp.max(large) > 0.5)
    def _():
        lax.fori_loop(0, number, by_maximum, 0)


def attend(slots, entry, x, keys, values_t, heads, qlength):
    number, _, head_size = x.shape
    context = keys.shape[1]
    tables = [] if isinstance(entry, int) else [slots]
    return pl.pallas_call(
        functools.partial(attend_kernel, entry=entry, heads=heads, qlength=qlength, chunk=512),
        in_specs=[VMEM] * (len(tables) + 3),
        out_specs=VMEM,
        out_shape=jax.ShapeDtypeStruct((number * qlength, heads * head_size), BF16),
        compiler_params=pltpu.CompilerParams(vmem_limit_bytes=20 << 20),
        cost_estimate=pl.CostEstimate(
            flops=8 * number * qlength * heads * context * head_size,
            bytes_accessed=4 << 20,
            transcendentals=number * qlength * heads * context,
        ),
        name="attend",
    )(*tables, x, keys, values_t)


def project_kernel(a_ref, w_ref, *out_refs, flips, tile):
    columns = out_refs[0].shape[1]
    me = lax.axis_index("tensor")

    def one(i, carry):
        out = pl.ds(pl.multiple_of(i * tile, tile), tile)
        for ref, flip in zip(out_refs, flips):
            source = pl.ds(pl.multiple_of((me ^ flip) * columns + i * tile, tile), tile)
            product = jnp.dot(a_ref[...], w_ref[:, source], preferred_element_type=F32)
            ref[:, out] = product.astype(ref.dtype)
        return carry

    lax.fori_loop(0, columns // tile, one, 0)


def project(rows, weight, shares, tile, flips, types):
    number, depth = rows.shape
    columns = weight.shape[1] // shares
    return pl.pallas_call(
        functools.partial(project_kernel, flips=flips, tile=tile),
        in_specs=[VMEM, VMEM],
        out_specs=[VMEM] * len(flips),
        out_shape=[jax.ShapeDtypeStruct((number, columns), kind) for kind in types],
        compiler_params=pltpu.CompilerParams(vmem_limit_bytes=12 << 20),
        cost_estimate=pl.CostEstimate(
            flops=2 * len(flips) * number * depth * columns,
            bytes_accessed=2 * len(flips) * depth * columns,
            transcendentals=0,
        ),
        name="project",
    )(rows, weight)


def finish_kernel(table_ref, kept_ref, core_ref, far_ref, *refs, first, qlength):
    o_ref, block_ref, sems = refs[-3:]
    number, _, columns = block_ref.shape
    t = lax.broadcasted_iota(jnp.int32, (qlength, columns), 0)
    copies = []
    for i in range(number):
        place = jnp.maximum(table_ref[first + i], 0)
        count = table_ref[table_ref.shape[0] // 2 + first + i]
        rows = slice(i * qlength, (i + 1) * qlength)
        total = kept_ref[rows, :] + core_ref[rows, :].astype(F32) + far_ref[rows, :].astype(F32)
        block_ref[i] = jnp.where(t < count, total, 0.0).astype(BF16)
        target = o_ref.at[pl.ds(pl.multiple_of(place * qlength, qlength), qlength), :]
        copies.append(pltpu.make_async_copy(block_ref.at[i], target, sems.at[i]))
        copies[-1].start()
    for copy in copies:
        copy.wait()


def finish(table, kept, from_core, from_far, first, previous, rows, qlength):
    number, columns = kept.shape[0] // qlength, kept.shape[1]
    extra = [] if previous is None else [pltpu.with_memory_space_constraint(previous, pltpu.HBM)]
    hbm = pl.BlockSpec(memory_space=pltpu.HBM)
    return pl.pallas_call(
        functools.partial(finish_kernel, first=first, qlength=qlength),
        in_specs=[SMEM, VMEM, VMEM, VMEM] + [hbm] * len(extra),
        out_specs=hbm,
        out_shape=pltpu.HBM((rows, columns), BF16),
        scratch_shapes=[pltpu.VMEM((number, qlength, columns), BF16), pltpu.SemaphoreType.DMA((number,))],
        input_output_aliases={4: 0} if extra else {},
        compiler_params=pltpu.CompilerParams(vmem_limit_bytes=12 << 20),
        cost_estimate=pl.CostEstimate(flops=0, bytes_accessed=10 * kept.shape[0] * columns, transcendentals=0),
        name="finish",
    )(table, kept, from_core, from_far, *extra)


def by_shift(shift, replicas):
    return [(i, (i + shift) % replicas) for i in range(replicas)]


def small_slice(groups, replicas, shares):
    return groups <= 2 and replicas == 4 and shares == 4


def project_out(table, results, weight, shares, first, out, rows, qlength):
    other_core = [(i, i ^ 1) for i in range(shares)]
    other_chip = [(i, i ^ 2) for i in range(shares)]
    tile = 512
    far_give, far_keep = project(results, weight, shares, tile, (3, 2), (BF16, F32))
    far_core = lax.ppermute(far_give, "tensor", other_core)
    (near_give,) = project(results, weight, shares, tile, (1,), (BF16,))
    near_core = lax.ppermute(near_give, "tensor", other_core)
    chip_sum = (far_keep + far_core.astype(F32)).astype(BF16)
    far = lax.ppermute(chip_sum, "tensor", other_chip)
    (near_keep,) = project(results, weight, shares, tile, (0,), (F32,))
    return finish(table, near_keep, near_core, far, first, out, rows, qlength)


def answer_by_first_slots(queries, own, pairs, context, stored, ids, counts, heads, qlength):
    replicas = stored.shape[1]
    route = functools.partial(route_first, replicas)
    table, _, _, packed, (keys, values_t) = pack(
        stored, ids, counts, queries, own, pairs, context, 1, replicas, route
    )
    arrived = [packed[0]] + [lax.ppermute(packed[s], "replica", by_shift(s, replicas)) for s in range(1, replicas)]
    result = attend(None, 0, jnp.concatenate(arrived), keys, values_t, heads, qlength)
    parts = result.reshape(replicas, CAP * qlength, -1)
    returned = [parts[0]] + [lax.ppermute(parts[s], "replica", by_shift(-s, replicas)) for s in range(1, replicas)]
    return table, jnp.concatenate(returned)


def on_device(queries, new_kv, cache_kv, stored, haystack_ids, token_counts, out_weight):
    groups = lax.axis_size("groups")
    replicas = lax.axis_size("replica")
    shares = lax.axis_size("tensor")
    slots, context = cache_kv.shape[:2]
    head_size = cache_kv.shape[-1]
    questions = haystack_ids.shape[0]
    rows = queries.shape[0]
    qlength = rows // questions
    heads = queries.shape[1] // head_size
    own = new_kv.reshape(2 * rows, head_size)
    pairs = cache_kv.reshape(-1, head_size)
    ids = haystack_ids.T
    stored = stored.T

    if small_slice(groups, replicas, shares) and replicas * CAP == questions and slots == 2:
        table, failed, chosen, packed, (keys, values_t) = pack(
            stored, ids, token_counts, queries, own, pairs, context, slots, 4, route_near
        )
        arrived, returned = dict(enumerate(packed)), {}
        shifts = {2: 1, 3: -1}
        for s, shift in shifts.items():
            arrived[s] = lax.ppermute(packed[s], "replica", by_shift(shift, replicas))
        for s in range(4):
            if s == 1:
                keys, values_t = split(pairs, keys, values_t, 1, returned[0])
            returned[s] = attend(chosen, s if s < 2 else (s - 2,), arrived[s], keys, values_t, heads, qlength)
            if s in shifts:
                returned[s] = lax.ppermute(returned[s], "replica", by_shift(-shifts[s], replicas))
        out = None
        for s in range(4):
            out = project_out(table, returned[s], out_weight, shares, s * CAP, out, rows, qlength)

        def again():
            table, results = answer_by_first_slots(queries, own, pairs, context, stored, ids, token_counts, heads, qlength)
            return project_out(table, results, out_weight, shares, 0, None, rows, qlength)

        return lax.cond(failed[0] > 0, again, lambda: out)

    table, results = answer_by_first_slots(queries, own, pairs, context, stored, ids, token_counts, heads, qlength)
    blocks = results.reshape(replicas * CAP, qlength, -1)
    match = table[None, : replicas * CAP] == jnp.arange(questions, dtype=jnp.int32)[:, None]
    position = jnp.argmax(match.astype(jnp.int32), axis=1)
    used = jnp.arange(qlength, dtype=jnp.int32)[None, :] < token_counts[0][:, None]
    attended = jnp.where(used[..., None], blocks[position], jnp.zeros((), BF16)).reshape(rows, -1)
    summed = lax.psum_scatter(
        lax.dot_general(out_weight, attended, (((0,), (1,)), ((), ())), preferred_element_type=F32),
        "tensor",
        scatter_dimension=0,
        tiled=True,
    )
    return summed.T.astype(BF16)


def solution(mesh):
    in_specs = (
        P(("groups", "replica"), "tensor"),
        P(("groups", "replica"), None, "tensor"),
        P(("groups", "replica"), None, None, "tensor"),
        P("groups", None),
        P(("groups", "replica"), None),
        P(("groups", "replica"), None),
        P("tensor", None),
    )
    out_specs = P(("groups", "replica"), "tensor")
    return jax.shard_map(
        on_device, mesh=mesh, in_specs=in_specs, out_specs=out_specs, check_vma=False
    )
```

```python
import functools
import math

import jax
import jax.numpy as jnp
from jax import lax
from jax.experimental import pallas as pl
from jax.experimental.pallas import tpu as pltpu
from jax.sharding import PartitionSpec as P


CAP = 2
BF16 = jnp.bfloat16
F32 = jnp.float32
LOG2E = 1.4426950408889634
TOTAL_MAX = 1e30
VMEM = pl.BlockSpec(memory_space=pltpu.VMEM)
SMEM = pl.BlockSpec(memory_space=pltpu.SMEM)


def pack_kernel(
    stored_hbm, ids_hbm, counts_hbm, q_hbm, own_hbm, kv_hbm, table_ref, failed_ref, slots_ref, *refs, route, heads, qlength
):
    number = len(refs) - 11
    out_refs, (k_ref, vt_ref) = refs[:number], refs[number : number + 2]
    stored_ref, ids_ref, counts_ref, q_ref, own_ref, sems, pairs_ref, wide_ref, kv_sems = refs[number + 2 :]
    head_size = own_ref.shape[1]
    questions = ids_ref.shape[1]
    pairs = ((stored_hbm, stored_ref), (ids_hbm, ids_ref), (counts_hbm, counts_ref), (q_hbm, q_ref), (own_hbm, own_ref))
    copies = [pltpu.make_async_copy(source, target, sems.at[i]) for i, (source, target) in enumerate(pairs)]
    kv_copies = split_copies(kv_hbm, pairs_ref, kv_sems, 0)
    for copy in copies + kv_copies:
        copy.start()
    for copy in copies[:3]:
        copy.wait()
    places = []
    for s, haystack in enumerate(route(stored_ref, slots_ref, failed_ref)):
        count = jnp.int32(0)
        found = [jnp.int32(-1)] * CAP
        for i in range(questions):
            hit = ids_ref[0, i] == haystack
            for j in range(CAP):
                found[j] = jnp.where(hit & (count == j), jnp.int32(i), found[j])
            count = count + hit.astype(jnp.int32)
        for j in range(CAP):
            table_ref[s * CAP + j] = found[j]
        places.append([jnp.maximum(place, 0) for place in found])
        for j, place in enumerate(places[s]):
            table_ref[(number + s) * CAP + j] = counts_ref[0, place]
    for copy in copies[3:]:
        copy.wait()
    for s, out_ref in enumerate(out_refs):
        for j, place in enumerate(places[s]):
            rows = q_ref[pl.ds(pl.multiple_of(place * qlength, qlength), qlength), :]
            for h in range(heads):
                out_ref[j, h * qlength : (h + 1) * qlength, :] = rows[:, h * head_size : (h + 1) * head_size]
            own = own_ref[pl.ds(pl.multiple_of(place * 2 * qlength, 2 * qlength), 2 * qlength), :]
            out_ref[j, heads * qlength :, :] = own
    split_arrived(kv_copies, k_ref, vt_ref, pairs_ref, wide_ref, 0)


def route_first(replicas, stored_ref, slots_ref, failed_ref):
    failed_ref[0] = jnp.int32(0)
    slots_ref[...] = jnp.zeros_like(slots_ref)
    me = lax.axis_index("replica")
    return [stored_ref[0, lax.rem(me + s, replicas)] for s in range(replicas)]


def route_near(stored_ref, slots_ref, failed_ref):
    me = lax.axis_index("replica")

    def held(replica):
        return [stored_ref[slot, replica] for slot in range(2)]

    def plan(replica):
        here, after, before = [held(lax.rem(replica + d, 4)) for d in (0, 1, 3)]
        done = jnp.bool_(False)
        slots = [jnp.int32(0), jnp.int32(0)]
        chosen = [after[0], before[0]]
        for i in range(2):
            for k in range(2):
                one, two = after[i], before[k]
                fits = (one != here[0]) & (one != here[1]) & (two != here[0]) & (two != here[1]) & (one != two)
                take = fits & jnp.logical_not(done)
                slots = [jnp.where(take, i, slots[0]), jnp.where(take, k, slots[1])]
                chosen = [jnp.where(take, one, chosen[0]), jnp.where(take, two, chosen[1])]
                done = done | fits
        return slots, chosen, done

    plans = [plan(lax.rem(me + d, 4)) for d in range(4)]
    failed = jnp.int32(0)
    for _, _, done in plans:
        failed = jnp.where(done, failed, 1)
    for i, slot in enumerate((plans[3][0][0], plans[1][0][1])):
        slots_ref[i] = jnp.full(slots_ref.shape[1:], slot, jnp.int32).astype(F32)
    failed_ref[0] = failed
    return held(me) + plans[0][1]


def pack(stored, ids, counts, queries, own, pairs, context, slots, phases, route):
    questions = ids.shape[1]
    head_size = own.shape[1]
    qlength = queries.shape[0] // questions
    heads = queries.shape[1] // head_size
    rows = heads * qlength + 2 * qlength
    arguments = [pltpu.with_memory_space_constraint(x, pltpu.HBM) for x in (stored, ids, counts, queries, own, pairs)]
    split_out, split_scratch = split_shapes(context, head_size, slots)
    out = pl.pallas_call(
        functools.partial(pack_kernel, route=route, heads=heads, qlength=qlength),
        in_specs=[pl.BlockSpec(memory_space=pltpu.HBM)] * 6,
        out_specs=[SMEM, SMEM] + [VMEM] * (phases + 3),
        out_shape=[jax.ShapeDtypeStruct((size,), jnp.int32) for size in (2 * phases * CAP, 1)]
        + [jax.ShapeDtypeStruct((2, 8, 128), F32)]
        + [jax.ShapeDtypeStruct((CAP, rows, head_size), BF16)] * phases
        + split_out,
        scratch_shapes=[
            pltpu.SMEM(stored.shape, jnp.int32),
            pltpu.SMEM(ids.shape, jnp.int32),
            pltpu.SMEM(counts.shape, jnp.int32),
            pltpu.VMEM(queries.shape, BF16),
            pltpu.VMEM(own.shape, BF16),
            pltpu.SemaphoreType.DMA((5,)),
            *split_scratch,
        ],
        compiler_params=pltpu.CompilerParams(vmem_limit_bytes=16 << 20),
        cost_estimate=pl.CostEstimate(flops=0, bytes_accessed=4 << 20, transcendentals=0),
        name="pack",
    )(*arguments)
    return *out[:3], out[3:-2], out[-2:]


def split_copies(x_ref, pairs_ref, sems, slot):
    parts, block, _ = pairs_ref.shape
    return [
        pltpu.make_async_copy(x_ref.at[pl.ds((slot * parts + i) * block, block), :], pairs_ref.at[i], sems.at[i])
        for i in range(parts)
    ]


def split_arrived(copies, k_ref, vt_ref, pairs_ref, wide_ref, slot):
    half, head_size = pairs_ref.shape[1] // 2, pairs_ref.shape[2]
    depth, context = vt_ref.shape[1:]
    vt_ref[slot, head_size:, :] = jnp.ones((depth - head_size, context), BF16)
    for i, copy in enumerate(copies):
        copy.wait()
        wide = wide_ref.at[i % 2]
        wide[...] = pairs_ref[i].astype(F32)
        k_ref[slot, i * half : (i + 1) * half, :] = wide[pl.ds(0, half, stride=2), :].astype(BF16)
        values = wide[pl.ds(1, half, stride=2), :]
        vt_ref[slot, :head_size, i * half : (i + 1) * half] = values.T.astype(BF16)


def split_shapes(context, head_size, slots):
    parts = 8
    block = 2 * context // parts
    out_shape = [
        jax.ShapeDtypeStruct((slots, context, head_size), BF16),
        jax.ShapeDtypeStruct((slots, head_size + 16, context), BF16),
    ]
    scratch_shapes = [
        pltpu.VMEM((parts, block, head_size), BF16),
        pltpu.VMEM((2, block, head_size), F32),
        pltpu.SemaphoreType.DMA((parts,)),
    ]
    return out_shape, scratch_shapes


def split_kernel(x_ref, keys_ref, values_ref, after_ref, k_ref, vt_ref, pairs_ref, wide_ref, sems, *, slot):
    copies = split_copies(x_ref, pairs_ref, sems, slot)
    for copy in copies:
        copy.start()
    split_arrived(copies, k_ref, vt_ref, pairs_ref, wide_ref, slot)


def split(pairs, keys, values_t, slot, after):
    slots, context, head_size = keys.shape
    out_shape, scratch_shapes = split_shapes(context, head_size, slots)
    hbm = pl.BlockSpec(memory_space=pltpu.HBM)
    return pl.pallas_call(
        functools.partial(split_kernel, slot=slot),
        in_specs=[hbm, VMEM, VMEM, pl.BlockSpec(memory_space=pl.ANY)],
        out_specs=[VMEM, VMEM],
        out_shape=out_shape,
        scratch_shapes=scratch_shapes,
        input_output_aliases={1: 0, 2: 1},
        compiler_params=pltpu.CompilerParams(vmem_limit_bytes=16 << 20),
        cost_estimate=pl.CostEstimate(flops=0, bytes_accessed=8 * context * head_size, transcendentals=0),
        name="split",
    )(pltpu.with_memory_space_constraint(pairs, pltpu.HBM), keys, values_t, after)


def attend_kernel(*refs, entry, heads, qlength, chunk):
    if isinstance(entry, int):
        x_ref, keys_ref, values_ref, o_ref = refs
        slot = entry
    else:
        slots_ref, x_ref, keys_ref, values_ref, o_ref = refs
        slot = jnp.max(slots_ref[entry[0]]).astype(jnp.int32)
    k_ref, vt_ref = keys_ref.at[slot], values_ref.at[slot]
    context, head_size = k_ref.shape
    scale = LOG2E / math.sqrt(head_size)
    rows = heads * qlength

    def start(i):
        qt = x_ref[i, :rows, :].T
        own = x_ref[i, rows:, :]
        near = jnp.dot(own, qt, preferred_element_type=F32) * scale
        u2 = lax.broadcasted_iota(jnp.int32, near.shape, 0)
        t = lax.broadcasted_iota(jnp.int32, near.shape, 1) % qlength
        near = jnp.where((u2 % 2 == 0) & (u2 <= 2 * t), near, -jnp.inf)
        own_vt = jnp.concatenate([own.astype(F32).T.astype(BF16), jnp.ones((16, own.shape[0]), BF16)], axis=0)

        def mix_near(top):
            weights = pltpu.roll(jnp.exp2(near - top), 1, 0).astype(BF16)
            return jnp.dot(own_vt, weights, preferred_element_type=F32)

        return qt, jnp.max(near, axis=0, keepdims=True), mix_near

    def store(i, mixed):
        result = (mixed[:head_size] / mixed[head_size : head_size + 1]).T.astype(BF16)
        target = pl.ds(i * qlength if isinstance(i, int) else pl.multiple_of(i * qlength, qlength), qlength)
        for h in range(heads):
            o_ref[target, h * head_size : (h + 1) * head_size] = result[h * qlength : (h + 1) * qlength, :]

    def shifted(i):
        qt, top, mix_near = start(i)
        scores = jnp.dot(k_ref[...], qt, preferred_element_type=F32) * scale
        weights = jnp.exp2(scores - top).astype(BF16)
        mixed = jnp.dot(vt_ref[...], weights, preferred_element_type=F32) + mix_near(top)
        store(i, mixed)
        return jnp.where(mixed[head_size : head_size + 1] < TOTAL_MAX, 0.0, 1.0)

    def by_maximum(i, carry):
        qt, top, mix_near = start(i)

        def part(j):
            keys = k_ref[pl.ds(pl.multiple_of(j * chunk, chunk), chunk), :]
            return jnp.dot(keys, qt, preferred_element_type=F32) * scale

        def raise_top(j, top):
            return jnp.maximum(top, jnp.max(part(j), axis=0, keepdims=True))

        top = lax.fori_loop(0, context // chunk, raise_top, top)

        def add(j, mixed):
            weights = jnp.exp2(part(j) - top).astype(BF16)
            values = vt_ref[:, pl.ds(pl.multiple_of(j * chunk, chunk), chunk)]
            return mixed + jnp.dot(values, weights, preferred_element_type=F32)

        store(i, lax.fori_loop(0, context // chunk, add, mix_near(top)))
        return carry

    number = x_ref.shape[0]
    if number == CAP:
        large = functools.reduce(jnp.maximum, [shifted(i) for i in range(number)])
    else:
        large = lax.fori_loop(0, number, lambda i, large: jnp.maximum(large, shifted(i)), jnp.zeros((1, rows), F32))

    @pl.when(jnp.max(large) > 0.5)
    def _():
        lax.fori_loop(0, number, by_maximum, 0)


def attend(slots, entry, x, keys, values_t, heads, qlength):
    number, _, head_size = x.shape
    context = keys.shape[1]
    tables = [] if isinstance(entry, int) else [slots]
    return pl.pallas_call(
        functools.partial(attend_kernel, entry=entry, heads=heads, qlength=qlength, chunk=512),
        in_specs=[VMEM] * (len(tables) + 3),
        out_specs=VMEM,
        out_shape=jax.ShapeDtypeStruct((number * qlength, heads * head_size), BF16),
        compiler_params=pltpu.CompilerParams(vmem_limit_bytes=20 << 20),
        cost_estimate=pl.CostEstimate(
            flops=8 * number * qlength * heads * context * head_size,
            bytes_accessed=4 << 20,
            transcendentals=number * qlength * heads * context,
        ),
        name="attend",
    )(*tables, x, keys, values_t)


def project_kernel(a_ref, w_ref, *out_refs, flips, tile):
    columns = out_refs[0].shape[1]
    me = lax.axis_index("tensor")

    def one(i, carry):
        out = pl.ds(pl.multiple_of(i * tile, tile), tile)
        for ref, flip in zip(out_refs, flips):
            source = pl.ds(pl.multiple_of((me ^ flip) * columns + i * tile, tile), tile)
            product = jnp.dot(a_ref[...], w_ref[:, source], preferred_element_type=F32)
            ref[:, out] = product.astype(ref.dtype)
        return carry

    lax.fori_loop(0, columns // tile, one, 0)


def project(rows, weight, shares, tile, flips, types):
    number, depth = rows.shape
    columns = weight.shape[1] // shares
    return pl.pallas_call(
        functools.partial(project_kernel, flips=flips, tile=tile),
        in_specs=[VMEM, VMEM],
        out_specs=[VMEM] * len(flips),
        out_shape=[jax.ShapeDtypeStruct((number, columns), kind) for kind in types],
        compiler_params=pltpu.CompilerParams(vmem_limit_bytes=12 << 20),
        cost_estimate=pl.CostEstimate(
            flops=2 * len(flips) * number * depth * columns,
            bytes_accessed=2 * len(flips) * depth * columns,
            transcendentals=0,
        ),
        name="project",
    )(rows, weight)


def finish_kernel(table_ref, kept_ref, core_ref, far_ref, *refs, first, qlength):
    o_ref, block_ref, sems = refs[-3:]
    number, _, columns = block_ref.shape
    t = lax.broadcasted_iota(jnp.int32, (qlength, columns), 0)
    copies = []
    for i in range(number):
        place = jnp.maximum(table_ref[first + i], 0)
        count = table_ref[table_ref.shape[0] // 2 + first + i]
        rows = slice(i * qlength, (i + 1) * qlength)
        total = kept_ref[rows, :] + core_ref[rows, :].astype(F32) + far_ref[rows, :].astype(F32)
        block_ref[i] = jnp.where(t < count, total, 0.0).astype(BF16)
        target = o_ref.at[pl.ds(pl.multiple_of(place * qlength, qlength), qlength), :]
        copies.append(pltpu.make_async_copy(block_ref.at[i], target, sems.at[i]))
        copies[-1].start()
    for copy in copies:
        copy.wait()


def finish(table, kept, from_core, from_far, first, previous, rows, qlength):
    number, columns = kept.shape[0] // qlength, kept.shape[1]
    extra = [] if previous is None else [pltpu.with_memory_space_constraint(previous, pltpu.HBM)]
    hbm = pl.BlockSpec(memory_space=pltpu.HBM)
    return pl.pallas_call(
        functools.partial(finish_kernel, first=first, qlength=qlength),
        in_specs=[SMEM, VMEM, VMEM, VMEM] + [hbm] * len(extra),
        out_specs=hbm,
        out_shape=pltpu.HBM((rows, columns), BF16),
        scratch_shapes=[pltpu.VMEM((number, qlength, columns), BF16), pltpu.SemaphoreType.DMA((number,))],
        input_output_aliases={4: 0} if extra else {},
        compiler_params=pltpu.CompilerParams(vmem_limit_bytes=12 << 20),
        cost_estimate=pl.CostEstimate(flops=0, bytes_accessed=10 * kept.shape[0] * columns, transcendentals=0),
        name="finish",
    )(table, kept, from_core, from_far, *extra)


def by_shift(shift, replicas):
    return [(i, (i + shift) % replicas) for i in range(replicas)]


def small_slice(groups, replicas, shares):
    return groups <= 2 and replicas == 4 and shares == 4


def project_out(label, table, results, weight, shares, first, out, rows, qlength):
    other_core = [(i, i ^ 1) for i in range(shares)]
    other_chip = [(i, i ^ 2) for i in range(shares)]
    tile = 512
    if label in (2, 3):
        (far_give,) = project(results, weight, shares, tile, (3,), (BF16,))
        (far_keep,) = project(results, weight, shares, tile, (2,), (F32,))
    else:
        far_give, far_keep = project(results, weight, shares, tile, (3, 2), (BF16, F32))
    far_core = lax.ppermute(far_give, "tensor", other_core)
    (near_give,) = project(results, weight, shares, tile, (1,), (BF16,))
    near_core = lax.ppermute(near_give, "tensor", other_core)
    chip_sum = (far_keep + far_core.astype(F32)).astype(BF16)
    far = lax.ppermute(chip_sum, "tensor", other_chip)
    (near_keep,) = project(results, weight, shares, tile, (0,), (F32,))
    return finish(table, near_keep, near_core, far, first, out, rows, qlength)


def answer_by_first_slots(queries, own, pairs, context, stored, ids, counts, heads, qlength):
    replicas = stored.shape[1]
    route = functools.partial(route_first, replicas)
    table, _, _, packed, (keys, values_t) = pack(
        stored, ids, counts, queries, own, pairs, context, 1, replicas, route
    )
    arrived = [packed[0]] + [lax.ppermute(packed[s], "replica", by_shift(s, replicas)) for s in range(1, replicas)]
    result = attend(None, 0, jnp.concatenate(arrived), keys, values_t, heads, qlength)
    parts = result.reshape(replicas, CAP * qlength, -1)
    returned = [parts[0]] + [lax.ppermute(parts[s], "replica", by_shift(-s, replicas)) for s in range(1, replicas)]
    return table, jnp.concatenate(returned)


def on_device(queries, new_kv, cache_kv, stored, haystack_ids, token_counts, out_weight):
    groups = lax.axis_size("groups")
    replicas = lax.axis_size("replica")
    shares = lax.axis_size("tensor")
    slots, context = cache_kv.shape[:2]
    head_size = cache_kv.shape[-1]
    questions = haystack_ids.shape[0]
    rows = queries.shape[0]
    qlength = rows // questions
    heads = queries.shape[1] // head_size
    own = new_kv.reshape(2 * rows, head_size)
    pairs = cache_kv.reshape(-1, head_size)
    ids = haystack_ids.T
    stored = stored.T

    if small_slice(groups, replicas, shares) and replicas * CAP == questions and slots == 2:
        table, failed, chosen, packed, (keys, values_t) = pack(
            stored, ids, token_counts, queries, own, pairs, context, slots, 4, route_near
        )
        arrived, returned = dict(enumerate(packed)), {}
        shifts = {2: 1, 3: -1}
        for s, shift in shifts.items():
            arrived[s] = lax.ppermute(packed[s], "replica", by_shift(shift, replicas))
        for s in range(4):
            if s == 1:
                keys, values_t = split(pairs, keys, values_t, 1, returned[0])
            returned[s] = attend(chosen, s if s < 2 else (s - 2,), arrived[s], keys, values_t, heads, qlength)
            if s in shifts:
                returned[s] = lax.ppermute(returned[s], "replica", by_shift(-shifts[s], replicas))
        out = None
        for s in range(4):
            out = project_out(
                s, table, returned[s], out_weight, shares, s * CAP, out, rows, qlength
            )

        def again():
            table, results = answer_by_first_slots(queries, own, pairs, context, stored, ids, token_counts, heads, qlength)
            return project_out(
                "again", table, results, out_weight, shares, 0, None, rows, qlength
            )

        return lax.cond(failed[0] > 0, again, lambda: out)

    table, results = answer_by_first_slots(queries, own, pairs, context, stored, ids, token_counts, heads, qlength)
    blocks = results.reshape(replicas * CAP, qlength, -1)
    match = table[None, : replicas * CAP] == jnp.arange(questions, dtype=jnp.int32)[:, None]
    position = jnp.argmax(match.astype(jnp.int32), axis=1)
    used = jnp.arange(qlength, dtype=jnp.int32)[None, :] < token_counts[0][:, None]
    attended = jnp.where(used[..., None], blocks[position], jnp.zeros((), BF16)).reshape(rows, -1)
    summed = lax.psum_scatter(
        lax.dot_general(out_weight, attended, (((0,), (1,)), ((), ())), preferred_element_type=F32),
        "tensor",
        scatter_dimension=0,
        tiled=True,
    )
    return summed.T.astype(BF16)


def solution(mesh):
    in_specs = (
        P(("groups", "replica"), "tensor"),
        P(("groups", "replica"), None, "tensor"),
        P(("groups", "replica"), None, None, "tensor"),
        P("groups", None),
        P(("groups", "replica"), None),
        P(("groups", "replica"), None),
        P("tensor", None),
    )
    out_specs = P(("groups", "replica"), "tensor")
    return jax.shard_map(
        on_device, mesh=mesh, in_specs=in_specs, out_specs=out_specs, check_vma=False
    )
```
